32 devices in a mesh: rep: 4 (over y, core), fsdp: 8 (over z, x).
Axes of the slice: x: 2, y: 2, z: 4, core: 2. Of those that a mesh axis runs over, the one named last changes fastest.
Arguments:
- query_cache: bfloat16 [1536, 4096], P(('rep', 'fsdp')), may hold values from -60 to 60
- passage_cache: bfloat16 [192, 4096], P(('rep', 'fsdp')), may hold values from -4 to 4
- positives: int32 [1536], P(('rep', 'fsdp')), may hold values from 0 to 191
- norm_gain: float32 [4096], P('fsdp'), may hold values from 0.1 to 1.9
- hidden_states: bfloat16 [8192, 4096], P(('rep', 'fsdp')), may hold values from -6 to 6
Outputs:
- loss: float32 [], replicated
- passage_grad: float32 [192, 4096], P(('rep', 'fsdp'))
- hidden_grad: bfloat16 [8192, 4096], P(('rep', 'fsdp'))
- gain_grad: float32 [4096], P('fsdp')
The draws below stay inside these ranges and needn't reach their ends.
All inputs are finite; a program needn't handle non-finite values.
Results may differ from the reference program's by a relative error of at most 0.0045.
The reference program's roundings to bfloat16 on the way (of `q_unit`, `p_unit` and `weights`) count: a program that leaves them out, or rounds other values in their place, can miss the bound.
Values may be sent and summed in bfloat16 or wider, within the bound.
A program may use at most 64 MiB of HBM per device.

```python
import jax
import jax.numpy as jnp
from jax import lax

D = 4096
PAS_DEV = 6
LEN = 256
NQ = 1536
NP = 192
N_REP = 4
DEVICES = 32


def draw_caches(key):
    key_query = jax.random.fold_in(key, 101)
    key_passage = jax.random.fold_in(key, 202)
    queries = jax.random.normal(key_query, (NQ, D), jnp.float32)
    passages = jax.random.normal(key_passage, (NP, D), jnp.float32) * 0.0625
    queries = jnp.clip(queries, -60.0, 60.0)
    passages = jnp.clip(passages, -4.0, 4.0)
    return (queries, passages)


def draw_query_cache(key, part):
    return draw_caches(key)[0].astype(jnp.bfloat16)


def draw_passage_cache(key, part):
    return draw_caches(key)[1].astype(jnp.bfloat16)


def place_ends(drawn, key, least, high):
    spot = [jax.random.randint(jax.random.fold_in(key, axis), (), 0, length) for axis, length in enumerate(drawn.shape)]
    longest = drawn.shape.index(max(drawn.shape))
    neighbour = spot[:longest] + [(spot[longest] + 1) % drawn.shape[longest]] + spot[longest + 1:]
    return drawn.at[tuple(spot)].set(least).at[tuple(neighbour)].set(high)


def with_spikes(array, own_key, source, target, blocks, factor):
    owner, partner = [(jnp.arange(array.shape[axis_at]) // (array.shape[axis_at] // blocks)).reshape([-1 if axis == axis_at else 1 for axis in range(array.ndim)]) for axis_at in (source, target)]
    chosen = jax.random.permutation(own_key, blocks)[partner]
    strong = (owner == chosen) | (owner == (partner + blocks // 2) % blocks)
    return jnp.where(strong, factor * array, array)


def block_levels(rng, shape, shards, low, top_value):
    factor_of, own = 1.0, jax.random.fold_in(rng, 6)
    for axis_at, parts in shards:
        steps = jnp.exp(jax.random.uniform(jax.random.fold_in(own, axis_at), (parts,), jnp.float32, low / len(shards), top_value / len(shards)))
        factor_of = factor_of * jnp.repeat(steps, shape[axis_at] // parts).reshape([-1 if axis == axis_at else 1 for axis in range(len(shape))])
    return factor_of


def noise_with(stream_key, shape, spread, reach, shards, heavy, kind=jnp.bfloat16):
    array = spread * jax.random.normal(stream_key, shape, jnp.float32)
    if shards:
        array = array * block_levels(stream_key, shape, shards, -0.22, 0.18)
    return jnp.clip(with_spikes(array, jax.random.fold_in(stream_key, 3), *heavy), -reach, reach).astype(kind)


def setup_inputs(seed: int = 0) -> dict:
    seeds = jax.random.split(jax.random.key(seed), 6)
    return {
        "query_cache": draw_query_cache(jax.random.fold_in(seeds[5], 71), 0),
        "passage_cache": draw_passage_cache(jax.random.fold_in(seeds[5], 71), 0),
        "positives": place_ends(jax.random.randint(seeds[2], (NQ,), 0, NP), jax.random.fold_in(seeds[2], 1), 0, NP - 1).astype(jnp.int32),
        "norm_gain": jnp.clip(1.0 + 0.18 * jax.random.normal(seeds[3], (D,), jnp.float32), 0.1, 1.9),
        "hidden_states": noise_with(seeds[4], (DEVICES * LEN, D), 1.0, 6.0, ((0, 32),), (0, 1, 32, 2.75)),
    }


score_scale = 256.0

def unit_rows(rows_in):
    widened = rows_in.astype(jnp.float32)
    radius = jnp.sqrt(lax.optimization_barrier(jnp.sum(widened * widened, axis=-1, keepdims=True)) + 1e-06)
    return (widened / radius, radius)

def local_backward(rows_in, top_row, gain_full):
    widened = rows_in.astype(jnp.float32)
    root_ms = jnp.sqrt(lax.optimization_barrier(jnp.mean(widened * widened, axis=-1, keepdims=True)) + 1e-05)
    inverse = 1.0 / root_ms
    slope_row = top_row / rows_in.shape[0]
    gain_term = slope_row * lax.optimization_barrier(jnp.sum(widened * inverse, axis=0))
    scaled = gain_full * slope_row
    inner_sum = jnp.dot(widened, scaled, precision=lax.Precision.HIGHEST)[:, None]
    grad_rows = scaled[None, :] * inverse - widened * inner_sum * (inverse * inverse * inverse) / rows_in.shape[1]
    return (grad_rows.astype(jnp.bfloat16), gain_term)

def reference(query_cache, passage_cache, positives, norm_gain, hidden_states):
    query_dir, query_radius = unit_rows(query_cache)
    q_unit = query_dir.astype(jnp.bfloat16)
    p_dir, p_radius = unit_rows(passage_cache)
    p_unit = p_dir.astype(jnp.bfloat16)
    pass_ids = jnp.arange(NP, dtype=jnp.int32)
    block_rows = NQ // N_REP

    def block_step(carried, paired):
        grad_sum, loss_sum = carried
        q_rows, pos_rows = paired
        scores = lax.dot_general(p_unit, q_rows, (((1,), (1,)), ((), ())), preferred_element_type=jnp.float32) * score_scale
        col_top = lax.optimization_barrier(jnp.max(scores, axis=0))
        log_total = col_top + jnp.log(lax.optimization_barrier(jnp.sum(jnp.exp(scores - col_top[None, :]), axis=0)))
        matches = (pass_ids[:, None] == pos_rows[None, :]).astype(jnp.float32)
        weights = (jnp.exp(scores - log_total[None, :]) - matches).astype(jnp.bfloat16)
        grad_sum = grad_sum + score_scale * jnp.dot(weights, q_rows, preferred_element_type=jnp.float32)
        loss_sum = loss_sum + jnp.sum(log_total) - jnp.sum(scores * matches)
        return ((grad_sum, loss_sum), None)
    initial = (jnp.zeros((NP, D), jnp.float32), jnp.zeros((), jnp.float32))
    (unit_grad, loss_sum), _ = lax.scan(block_step, initial, (q_unit.reshape(N_REP, block_rows, D), positives.reshape(N_REP, block_rows)))
    passage_grad = (unit_grad - p_dir * lax.optimization_barrier(jnp.sum(p_dir * unit_grad, axis=-1, keepdims=True))) / p_radius
    loss = loss_sum / NQ
    top_grad = passage_grad.reshape(DEVICES, PAS_DEV, D)[:, 0, :]
    blocks_in = hidden_states.reshape(DEVICES, LEN, D)

    def recompute(paired):
        return local_backward(paired[0], paired[1], norm_gain)
    hidden_grad, gain_terms = lax.map(recompute, (blocks_in, top_grad))
    gain_grad = lax.optimization_barrier(jnp.sum(gain_terms, axis=0))
    return (loss, passage_grad, hidden_grad.reshape(DEVICES * LEN, D), gain_grad)
```

```python
import functools

import jax
import jax.numpy as jnp
from jax import lax
from jax.experimental import pallas as pl
from jax.experimental.pallas import tpu as pltpu
from jax.sharding import PartitionSpec as P

score_scale = 256.0
PAD = 8
LANES = 128
GROUPS = 4
F32 = jnp.float32
BF16 = jnp.bfloat16


def remote(src, dst, send_sem, recv_sem, **where):
    return pltpu.make_async_remote_copy(
        src_ref=src,
        dst_ref=dst,
        send_sem=send_sem,
        recv_sem=recv_sem,
        device_id=where,
        device_id_type=pl.DeviceIdType.MESH,
    )


def kernel(
    n_rep, n_fsdp, q_hbm, p_hbm, pos_ref, gain_ref, h_hbm,
    loss_out, pg_out, h_out, gg_out,
    q_in, p_in, h_in, q_all, p_all, p_dir, pos_all, gain_all, scores, stat_all,
    a_all, top_send, top_recv, near_send, near_recv, far_send, far_recv, grad_own, unit_sum,
    share_send, share_recv, total_all, col_acc, row_inv, wide,
    in_sem, q_send, q_near, q_mate, q_far, p_send, p_near, p_far, pos_sem, gain_sem, a_sem,
    stat_sem, top_sem, share_sem, total_sem, near_sent, near_got, far_sem,
):
    rep, fsdp = lax.axis_index("rep"), lax.axis_index("fsdp")
    qry, dim = q_in.shape
    pas = p_in.shape[0]
    length = h_in.shape[0]
    half = n_rep // 2
    p_half = n_fsdp // 2
    part = dim // n_fsdp
    width = dim // GROUPS
    mate = rep + 1 - 2 * (rep % 2)
    p_mate = fsdp + 1 - 2 * (fsdp % 2)

    barrier = pltpu.get_barrier_semaphore()
    for k in range(1, n_rep):
        pl.semaphore_signal(barrier, inc=1, device_id={"rep": (rep + k) % n_rep},
                            device_id_type=pl.DeviceIdType.MESH)
    for k in range(1, n_fsdp):
        pl.semaphore_signal(barrier, inc=1, device_id={"fsdp": (fsdp + k) % n_fsdp},
                            device_id_type=pl.DeviceIdType.MESH)

    loads = [
        pltpu.make_async_copy(q_hbm, q_in, in_sem.at[0]),
        pltpu.make_async_copy(p_hbm, p_in, in_sem.at[1]),
        pltpu.make_async_copy(pos_ref, pos_all.at[rep], in_sem.at[2]),
        pltpu.make_async_copy(gain_ref, gain_all.at[fsdp], in_sem.at[3]),
        pltpu.make_async_copy(h_hbm, h_in, in_sem.at[4]),
    ]
    for load in loads:
        load.start()

    def who(j):
        return ((fsdp + 2 * j) if j < p_half else (p_mate + 2 * (j - p_half))) % n_fsdp

    def mirror(j):
        return (-j) % p_half if j < p_half else p_half + (-(j - p_half)) % p_half

    loads[0].wait()
    for c in range(qry // 16):
        rows = slice(c * 16, (c + 1) * 16)
        raw = q_in[rows, :].astype(F32)
        radius = jnp.sqrt(jnp.sum(raw * raw, axis=-1, keepdims=True) + 1e-06)
        q_all[0, rows, :] = (q_in[rows, :].astype(F32) * (1.0 / radius)).astype(BF16)

    loads[1].wait()
    wide_p = p_in[...].astype(F32)
    p_radius = jnp.sqrt(jnp.sum(wide_p * wide_p, axis=-1, keepdims=True) + 1e-06)
    p_inv = 1.0 / p_radius
    p_dir[...] = wide_p * p_inv
    p_all[0] = jnp.concatenate([p_dir[...], jnp.zeros((PAD - pas, dim), F32)], axis=0).astype(BF16)

    pl.semaphore_wait(barrier, n_rep + n_fsdp - 2)

    def cols_of(g):
        return slice(g * width, (g + 1) * width)

    def p_block(j):
        return p_all.at[j, 0:pas]

    for g in range(GROUPS):
        for k in range(1, half):
            remote(q_all.at[0, :, cols_of(g)], q_all.at[half - k, :, cols_of(g)], q_send,
                   q_near.at[half - k, g], rep=(rep + 2 * k) % n_rep).start()
        if g == 0:
            for k in range(1, p_half):
                remote(p_block(0), p_block(p_half - k), p_send, p_near.at[p_half - k],
                       fsdp=who(k)).start()
            remote(p_block(0), p_block(p_half), p_send, p_far, fsdp=p_mate).start()
    remote(q_all.at[0], q_all.at[half], q_send, q_mate, rep=mate).start()
    loads[2].wait()
    loads[3].wait()
    for k in range(1, n_rep):
        remote(pos_all.at[rep], pos_all.at[rep], pos_sem.at[0], pos_sem.at[1],
               rep=(rep + k) % n_rep).start()
    for k in range(1, n_fsdp):
        remote(gain_all.at[fsdp], gain_all.at[fsdp], gain_sem.at[0], gain_sem.at[1],
               fsdp=(fsdp + k) % n_fsdp).start()

    loads[4].wait()
    col_acc[...] = jnp.zeros_like(col_acc)

    def first_pass(i, _):
        rows = pl.ds(pl.multiple_of(i * 16, 16), 16)
        x = h_in[rows, :].astype(F32)
        inv = 1.0 / jnp.sqrt(jnp.sum(x * x, axis=-1, keepdims=True) / dim + 1e-05)
        row_inv[rows, :] = jnp.broadcast_to(inv, (16, LANES))
        y = h_in[rows, :].astype(F32) * inv
        col_acc[...] += y[:8] + y[8:]
        return 0

    lax.fori_loop(0, length // 16, first_pass, 0)
    colsum = jnp.sum(col_acc[...], axis=0, keepdims=True)
    a_all[0] = colsum * (p_inv[0:1] / length)

    def q_forward(g):
        for k in range(1, half):
            ref = q_all.at[k, :, cols_of(g)]
            remote(ref, ref, q_send, q_near.at[k, g], rep=mate).wait_recv()
            remote(ref, q_all.at[half + k, :, cols_of(g)], q_send, q_far.at[k, g], rep=mate).start()

    def p_forward(k):
        remote(p_block(k), p_block(k), p_send, p_near.at[k], fsdp=p_mate).wait_recv()
        remote(p_block(k), p_block(p_half + k), p_send, p_far, fsdp=p_mate).start()

    p_forward(1)
    q_forward(0)
    for k in range(2, p_half):
        p_forward(k)
    for j in range(1, n_fsdp):
        remote(a_all.at[0], a_all.at[mirror(j)], a_sem.at[0], a_sem.at[1], fsdp=who(j)).start()
    for g in range(1, GROUPS - 1):
        q_forward(g)
    remote(p_all.at[0:p_half, 0:pas], p_all.at[p_half:n_fsdp, 0:pas], p_send, p_far,
           fsdp=p_mate).wait_recv()

    rows_all = n_fsdp * PAD
    slot = lax.broadcasted_iota(jnp.int32, (rows_all, qry), 0)
    lane = slot % PAD
    valid = lane < pas
    index = slot // PAD
    source = jnp.where(index < p_half, fsdp + 2 * index, p_mate + 2 * (index - p_half))
    source = jnp.where(source >= n_fsdp, source - n_fsdp, source)
    pass_ids = (rep * n_fsdp + source) * pas + lane

    order = [(rep + 2 * k) % n_rep for k in range(half)] + [(mate + 2 * k) % n_rep for k in range(half)]

    def product(i, g0, g1):
        cols = slice(g0 * width, g1 * width)
        return lax.dot_general(p_all[:, :, cols].reshape(rows_all, (g1 - g0) * width), q_all[i, :, cols],
                               (((1,), (1,)), ((), ())), preferred_element_type=F32)

    def finish(i, s):
        s = jnp.where(valid, s * score_scale, -1e30)
        scores[i] = s
        top = jnp.max(s, axis=0, keepdims=True)
        stat_all[rep, order[i], 0:1, 0:qry] = top
        stat_all[rep, order[i], 1:2, 0:qry] = jnp.sum(jnp.exp(s - top), axis=0, keepdims=True)

    stat_all[rep] = jnp.zeros(stat_all.shape[1:], F32)
    finish(0, product(0, 0, GROUPS))
    remote(q_all.at[0], q_all.at[half], q_send, q_mate, rep=mate).wait_recv()
    finish(half, product(half, 0, GROUPS))
    last = GROUPS - 1
    for k in range(1, half):
        for g in range(last):
            ref = q_all.at[half + k, :, cols_of(g)]
            remote(ref, ref, q_send, q_far.at[k, g], rep=mate).wait_recv()
    near_part = [product(k, 0, last) for k in range(1, half)]
    far_part = [product(half + k, 0, last) for k in range(1, half)]
    q_forward(last)
    for k in range(1, half):
        finish(k, near_part[k - 1] + product(k, last, GROUPS))
    for k in range(1, half):
        ref = q_all.at[half + k, :, cols_of(last)]
        remote(ref, ref, q_send, q_far.at[k, last], rep=mate).wait_recv()
        finish(half + k, far_part[k - 1] + product(half + k, last, GROUPS))

    for k in range(1, n_rep):
        remote(stat_all.at[rep], stat_all.at[rep], stat_sem.at[0], stat_sem.at[1],
               rep=(rep + k) % n_rep).start()
    others = pos_all.at[0:n_rep - 1]
    remote(others, others, pos_sem.at[0], pos_sem.at[1], rep=mate).wait()
    others = gain_all.at[0:n_fsdp - 1]
    remote(others, others, gain_sem.at[0], gain_sem.at[1], fsdp=p_mate).wait()
    remote(q_all.at[0:n_rep - 1], q_all.at[0:n_rep - 1], q_send, q_mate, rep=mate).wait_send()
    remote(p_all.at[0:n_fsdp - 1, 0:pas], p_all.at[0:n_fsdp - 1, 0:pas], p_send, p_far,
           fsdp=p_mate).wait_send()
    remote(a_all.at[1:n_fsdp], a_all.at[1:n_fsdp], a_sem.at[0], a_sem.at[1], fsdp=p_mate).wait()
    stats = stat_all.at[0:n_rep - 1]
    remote(stats, stats, stat_sem.at[0], stat_sem.at[1], rep=mate).wait()

    loss_part = jnp.zeros((1, 1), F32)
    weights = []
    for i, block in enumerate(order):
        tops = [stat_all[r, block, 0:1, 0:qry] for r in range(n_rep)]
        top = functools.reduce(jnp.maximum, tops)
        total = sum(stat_all[r, block, 1:2, 0:qry] * jnp.exp(tops[r] - top) for r in range(n_rep))
        log_total = top + jnp.log(total)
        s = scores[i]
        match = (pass_ids == pos_all[block]) & valid
        weights.append(jnp.exp(s - log_total) - jnp.where(match, 1.0, 0.0))
        hit = jnp.sum(jnp.where(match, s, 0.0), axis=0, keepdims=True)
        loss_part = loss_part - jnp.sum(hit, axis=1, keepdims=True)
        if i == 0:
            loss_part = loss_part + jnp.sum(log_total, axis=1, keepdims=True)
    weights = jnp.concatenate(weights, axis=1).astype(BF16)

    tile = min(1024, dim)
    for c in range(dim // tile):
        cols = slice(c * tile, (c + 1) * tile)
        grad = jnp.dot(weights, q_all[:, :, cols].reshape(n_rep * qry, tile),
                       preferred_element_type=F32) * score_scale
        grad_own[:, cols] = grad[0:p_half * PAD]
        for j in range(n_fsdp):
            top_send[j, :, cols] = grad[j * PAD:j * PAD + 1]
        for k in range(p_half):
            near_send[k, :, cols] = grad[(p_half + k) * PAD:(p_half + k + 1) * PAD].astype(BF16)

    passing = sorted(range(1, p_half), key=lambda k: abs(2 * k - p_half)) + [0]

    def near_copy(k):
        return remote(near_send.at[k, 0:pas], near_recv.at[k, 0:pas], near_sent, near_got.at[k],
                      fsdp=p_mate)

    for j in range(1, n_fsdp):
        remote(top_send.at[j], top_recv.at[mirror(j)], top_sem.at[0], top_sem.at[1],
               fsdp=who(j)).start()
    for k in passing:
        near_copy(k).start()

    gain_term = jnp.zeros((1, dim), F32)
    for j in range(n_fsdp):
        row = p_all[j, 0:1, :].astype(F32)
        own = top_send[j]
        inner = jnp.sum(row * own, axis=-1, keepdims=True)
        gain_term = gain_term + a_all[j] * (own - row * inner)
    for f in range(n_fsdp):
        share_send[f, :, 0:part] = gain_term[:, f * part:(f + 1) * part]
        share_send[f, :, part:] = jnp.broadcast_to(loss_part, (1, LANES))
    for j in range(1, n_fsdp):
        remote(share_send.at[who(j)], share_recv.at[mirror(j)], share_sem.at[0], share_sem.at[1],
               fsdp=who(j)).start()

    for k in passing:
        near_copy(k).wait_recv()
        both = grad_own[k * PAD:(k + 1) * PAD, :] + near_recv[k].astype(F32)
        if k:
            far_send[k] = both.astype(BF16)
            remote(far_send.at[k, 0:pas], far_recv.at[p_half - k, 0:pas], far_sem.at[0],
                   far_sem.at[1], fsdp=who(k)).start()
        else:
            unit_sum[...] = both

    remote(top_recv.at[1:n_fsdp], top_recv.at[1:n_fsdp], top_sem.at[0], top_sem.at[1],
           fsdp=p_mate).wait()
    top_grad = top_send[0]
    for j in range(1, n_fsdp):
        top_grad = top_grad + top_recv[j]
    row = p_dir[0:1, :]
    top_grad = (top_grad - row * jnp.sum(row * top_grad, axis=-1, keepdims=True)) * p_inv[0:1]
    slope = top_grad / length
    for f in range(n_fsdp):
        scaled = gain_all[f] * slope[:, f * part:(f + 1) * part]
        wide[:, f * part:(f + 1) * part] = jnp.broadcast_to(scaled, (16, part))

    remote(share_recv.at[1:n_fsdp], share_recv.at[1:n_fsdp], share_sem.at[0], share_sem.at[1],
           fsdp=p_mate).wait()
    share_recv[0] = share_send[fsdp]
    total_all[rep] = sum(share_recv[f] for f in range(n_fsdp))
    for k in range(1, n_rep):
        remote(total_all.at[rep], total_all.at[rep], total_sem.at[0], total_sem.at[1],
               rep=(rep + k) % n_rep).start()

    def last_pass(i, _):
        rows = pl.ds(pl.multiple_of(i * 16, 16), 16)
        inner = jnp.sum(h_in[rows, :].astype(F32) * wide[...], axis=-1, keepdims=True)
        inv = row_inv[rows, 0:1]
        coef = inner * (inv * inv * inv) / dim
        h_out[rows, :] = (wide[...] * inv - h_in[rows, :].astype(F32) * coef).astype(BF16)
        return 0

    lax.fori_loop(0, length // 16, last_pass, 0, unroll=2)

    totals = total_all.at[0:n_rep - 1]
    remote(totals, totals, total_sem.at[0], total_sem.at[1], rep=mate).wait()
    total = sum(total_all[r] for r in range(n_rep))
    gg_out[...] = total[:, 0:part]
    loss_out[...] = total[:, part:] / (qry * n_rep * n_fsdp)
    remote(near_send.at[:, 0:pas], near_recv.at[:, 0:pas], near_sent, near_got.at[0],
           fsdp=p_mate).wait_send()

    sums = far_recv.at[1:p_half, 0:pas]
    remote(sums, sums, far_sem.at[0], far_sem.at[1], fsdp=p_mate).wait()
    unit_grad = unit_sum[...]
    for k in range(1, p_half):
        unit_grad = unit_grad + far_recv[k].astype(F32)
    unit_grad = unit_grad[0:pas]
    rows_dir = p_dir[...]
    pg_out[...] = (
        unit_grad - rows_dir * jnp.sum(rows_dir * unit_grad, axis=-1, keepdims=True)) * p_inv
    pg_out[0:1, :] = top_grad


def write_out(*refs):
    count = (len(refs) - 1) // 2
    sems = refs[-1]
    copies = [pltpu.make_async_copy(refs[i], refs[count + i], sems.at[i]) for i in range(count)]
    for copy in copies:
        copy.start()
    for copy in copies:
        copy.wait()


def per_device(query_cache, passage_cache, positives, norm_gain, hidden_states):
    n_rep, n_fsdp = lax.axis_size("rep"), lax.axis_size("fsdp")
    qry, dim = query_cache.shape
    pas = passage_cache.shape[0]
    length = hidden_states.shape[0]
    part = dim // n_fsdp
    half, p_half = n_rep // 2, n_fsdp // 2
    vmem = pl.BlockSpec(memory_space=pltpu.VMEM)
    hbm = pl.BlockSpec(memory_space=pltpu.HBM)
    dma = pltpu.SemaphoreType.DMA
    results = pl.pallas_call(
        functools.partial(kernel, n_rep, n_fsdp),
        name="step",
        out_shape=(
            pltpu.VMEM((1, LANES), F32),
            pltpu.VMEM((pas, dim), F32),
            pltpu.VMEM((length, dim), BF16),
            pltpu.VMEM((1, part), F32),
        ),
        in_specs=[hbm] * 5,
        out_specs=(vmem, vmem, vmem, vmem),
        scratch_shapes=[
            pltpu.VMEM((qry, dim), BF16),
            pltpu.VMEM((pas, dim), BF16),
            pltpu.VMEM((length, dim), BF16),
            pltpu.VMEM((n_rep, qry, dim), BF16),
            pltpu.VMEM((n_fsdp, PAD, dim), BF16),
            pltpu.VMEM((pas, dim), F32),
            pltpu.VMEM((n_rep, 1, qry), jnp.int32),
            pltpu.VMEM((n_fsdp, 1, part), F32),
            pltpu.VMEM((n_rep, n_fsdp * PAD, qry), F32),
            pltpu.VMEM((n_rep, n_rep, 2, LANES), F32),
            pltpu.VMEM((n_fsdp, 1, dim), F32),
            pltpu.VMEM((n_fsdp, 1, dim), F32),
            pltpu.VMEM((n_fsdp, 1, dim), F32),
            pltpu.VMEM((p_half, PAD, dim), BF16),
            pltpu.VMEM((p_half, PAD, dim), BF16),
            pltpu.VMEM((p_half, PAD, dim), BF16),
            pltpu.VMEM((p_half, PAD, dim), BF16),
            pltpu.VMEM((p_half * PAD, dim), F32),
            pltpu.VMEM((PAD, dim), F32),
            pltpu.VMEM((n_fsdp, 1, part + LANES), F32),
            pltpu.VMEM((n_fsdp, 1, part + LANES), F32),
            pltpu.VMEM((n_rep, 1, part + LANES), F32),
            pltpu.VMEM((8, dim), F32),
            pltpu.VMEM((length, LANES), F32),
            pltpu.VMEM((16, dim), F32),
            dma((5,)),
            dma, dma((half, GROUPS)), dma, dma((half, GROUPS)),
            dma, dma((p_half,)), dma,
            dma((2,)), dma((2,)), dma((2,)), dma((2,)), dma((2,)), dma((2,)), dma((2,)),
            dma, dma((p_half,)), dma((2,)),
        ],
        compiler_params=pltpu.CompilerParams(
            collective_id=0, has_side_effects=True, vmem_limit_bytes=40 << 20),
    )(*[pltpu.with_memory_space_constraint(array, pltpu.HBM) for array in (
        query_cache, passage_cache, positives.reshape(1, qry), norm_gain.reshape(1, part),
        hidden_states)])
    loss, passage_grad, hidden_grad, gain_grad = pl.pallas_call(
        write_out,
        name="write_out",
        out_shape=tuple(pltpu.HBM(r.shape, r.dtype) for r in results),
        in_specs=[vmem] * 4,
        out_specs=(hbm,) * 4,
        scratch_shapes=[dma((4,))],
    )(*[pltpu.with_memory_space_constraint(r, pltpu.VMEM) for r in results])
    return loss[0, 0], passage_grad, hidden_grad, gain_grad.reshape(part)


def solution(mesh):
    return jax.shard_map(
        per_device,
        mesh=mesh,
        in_specs=(
            P(("rep", "fsdp"), None),
            P(("rep", "fsdp"), None),
            P(("rep", "fsdp")),
            P("fsdp"),
            P(("rep", "fsdp"), None),
        ),
        out_specs=(P(), P(("rep", "fsdp"), None), P(("rep", "fsdp"), None), P("fsdp")),
        check_vma=False,
    )
```

```python
import functools

import jax
import jax.numpy as jnp
from jax import lax
from jax.experimental import pallas as pl
from jax.experimental.pallas import tpu as pltpu
from jax.sharding import PartitionSpec as P

score_scale = 256.0
PAD = 8
LANES = 128
GROUPS = 4
F32 = jnp.float32
BF16 = jnp.bfloat16


def remote(src, dst, send_sem, recv_sem, **where):
    return pltpu.make_async_remote_copy(
        src_ref=src,
        dst_ref=dst,
        send_sem=send_sem,
        recv_sem=recv_sem,
        device_id=where,
        device_id_type=pl.DeviceIdType.MESH,
    )


def kernel(
    n_rep, n_fsdp, q_hbm, p_hbm, pos_ref, gain_ref, h_hbm,
    loss_out, pg_out, h_out, gg_out,
    q_in, p_in, h_in, q_all, p_all, p_dir, pos_all, gain_all, scores, stat_all,
    a_all, top_own, top_send, top_recv, near_send, near_recv, far_send, far_recv, grad_own,
    share_send, share_recv, total_all, col_acc, row_inv, wide,
    in_sem, q_send, q_near, q_mate, q_far, p_send, p_near, p_far, pos_sem, gain_sem, a_sem,
    stat_sem, top_sem, share_sem, total_sem, near_sent, near_got, far_sem,
):
    rep, fsdp = lax.axis_index("rep"), lax.axis_index("fsdp")
    qry, dim = q_in.shape
    pas = p_in.shape[0]
    length = h_in.shape[0]
    half = n_rep // 2
    p_half = n_fsdp // 2
    part = dim // n_fsdp
    width = dim // GROUPS
    mate = rep + 1 - 2 * (rep % 2)
    p_mate = fsdp + 1 - 2 * (fsdp % 2)
    odd = (fsdp // 2) % 2

    def turned(k):
        return odd * (p_half - k) + (1 - odd) * k

    barrier = pltpu.get_barrier_semaphore()
    for k in range(1, n_rep):
        pl.semaphore_signal(barrier, inc=1, device_id={"rep": (rep + k) % n_rep},
                            device_id_type=pl.DeviceIdType.MESH)
    for k in range(1, n_fsdp):
        pl.semaphore_signal(barrier, inc=1, device_id={"fsdp": (fsdp + k) % n_fsdp},
                            device_id_type=pl.DeviceIdType.MESH)

    loads = [
        pltpu.make_async_copy(q_hbm, q_in, in_sem.at[0]),
        pltpu.make_async_copy(p_hbm, p_in, in_sem.at[1]),
        pltpu.make_async_copy(pos_ref, pos_all.at[rep], in_sem.at[2]),
        pltpu.make_async_copy(gain_ref, gain_all.at[fsdp], in_sem.at[3]),
        pltpu.make_async_copy(h_hbm, h_in, in_sem.at[4]),
    ]
    for load in loads[:4]:
        load.start()

    def who(j):
        return ((fsdp + 2 * j) if j < p_half else (p_mate + 2 * (j - p_half))) % n_fsdp

    def mirror(j):
        return (-j) % p_half if j < p_half else p_half + (-(j - p_half)) % p_half

    loads[0].wait()
    for c in range(qry // 16):
        rows = slice(c * 16, (c + 1) * 16)
        raw = q_in[rows, :].astype(F32)
        radius = jnp.sqrt(jnp.sum(raw * raw, axis=-1, keepdims=True) + 1e-06)
        q_all[0, rows, :] = (q_in[rows, :].astype(F32) * (1.0 / radius)).astype(BF16)

    loads[1].wait()
    wide_p = p_in[...].astype(F32)
    p_radius = jnp.sqrt(jnp.sum(wide_p * wide_p, axis=-1, keepdims=True) + 1e-06)
    p_inv = 1.0 / p_radius
    p_dir[...] = wide_p * p_inv
    p_all[0] = jnp.concatenate([p_dir[...], jnp.zeros((PAD - pas, dim), F32)], axis=0).astype(BF16)

    loads[4].start()
    pl.semaphore_wait(barrier, n_rep + n_fsdp - 2)

    def cols_of(g):
        return slice(g * width, (g + 1) * width)

    def p_block(j):
        return p_all.at[j, 0:pas]

    for g in range(GROUPS):
        for k in range(1, half):
            remote(q_all.at[0, :, cols_of(g)], q_all.at[half - k, :, cols_of(g)], q_send,
                   q_near.at[half - k, g], rep=(rep + 2 * k) % n_rep).start()
        if g == 0:
            for k in range(1, p_half):
                k = turned(k)
                remote(p_block(0), p_block(p_half - k), p_send, p_near.at[p_half - k],
                       fsdp=(fsdp + 2 * k) % n_fsdp).start()
            remote(p_block(0), p_block(p_half), p_send, p_far, fsdp=p_mate).start()
    remote(q_all.at[0], q_all.at[half], q_send, q_mate, rep=mate).start()
    loads[2].wait()
    loads[3].wait()
    for k in range(1, n_rep):
        remote(pos_all.at[rep], pos_all.at[rep], pos_sem.at[0], pos_sem.at[1],
               rep=(rep + k) % n_rep).start()
    for k in range(1, n_fsdp):
        remote(gain_all.at[fsdp], gain_all.at[fsdp], gain_sem.at[0], gain_sem.at[1],
               fsdp=(fsdp + k) % n_fsdp).start()

    loads[4].wait()
    col_acc[...] = jnp.zeros_like(col_acc)

    def first_pass(i, _):
        rows = pl.ds(pl.multiple_of(i * 16, 16), 16)
        x = h_in[rows, :].astype(F32)
        inv = 1.0 / jnp.sqrt(jnp.sum(x * x, axis=-1, keepdims=True) / dim + 1e-05)
        row_inv[rows, :] = jnp.broadcast_to(inv, (16, LANES))
        y = h_in[rows, :].astype(F32) * inv
        col_acc[...] += y[:8] + y[8:]
        return 0

    lax.fori_loop(0, length // 16, first_pass, 0)
    colsum = jnp.sum(col_acc[...], axis=0, keepdims=True)
    a_all[0] = colsum * (p_inv[0:1] / length)

    def q_forward(g):
        for k in range(1, half):
            ref = q_all.at[k, :, cols_of(g)]
            remote(ref, ref, q_send, q_near.at[k, g], rep=mate).wait_recv()
            remote(ref, q_all.at[half + k, :, cols_of(g)], q_send, q_far.at[k, g], rep=mate).start()

    def p_forward(k):
        remote(p_block(k), p_block(k), p_send, p_near.at[k], fsdp=p_mate).wait_recv()
        remote(p_block(k), p_block(p_half + k), p_send, p_far, fsdp=p_mate).start()

    for k in range(1, p_half):
        p_forward(turned(k))
    q_forward(0)
    for j in range(1, n_fsdp):
        remote(a_all.at[0], a_all.at[mirror(j)], a_sem.at[0], a_sem.at[1], fsdp=who(j)).start()
    for g in range(1, GROUPS - 1):
        q_forward(g)
    remote(p_all.at[0:p_half, 0:pas], p_all.at[p_half:n_fsdp, 0:pas], p_send, p_far,
           fsdp=p_mate).wait_recv()

    rows_all = n_fsdp * PAD
    slot = lax.broadcasted_iota(jnp.int32, (rows_all, qry), 0)
    lane = slot % PAD
    valid = lane < pas
    index = slot // PAD
    source = jnp.where(index < p_half, fsdp + 2 * index, p_mate + 2 * (index - p_half))
    source = jnp.where(source >= n_fsdp, source - n_fsdp, source)
    pass_ids = (rep * n_fsdp + source) * pas + lane

    order = [(rep + 2 * k) % n_rep for k in range(half)] + [(mate + 2 * k) % n_rep for k in range(half)]

    def product(i, g0, g1):
        cols = slice(g0 * width, g1 * width)
        return lax.dot_general(p_all[:, :, cols].reshape(rows_all, (g1 - g0) * width), q_all[i, :, cols],
                               (((1,), (1,)), ((), ())), preferred_element_type=F32)

    def finish(i, s):
        s = jnp.where(valid, s * score_scale, -1e30)
        scores[i] = s
        top = jnp.max(s, axis=0, keepdims=True)
        stat_all[rep, order[i], 0:1, 0:qry] = top
        stat_all[rep, order[i], 1:2, 0:qry] = jnp.sum(jnp.exp(s - top), axis=0, keepdims=True)

    stat_all[rep] = jnp.zeros(stat_all.shape[1:], F32)
    finish(0, product(0, 0, GROUPS))
    remote(q_all.at[0], q_all.at[half], q_send, q_mate, rep=mate).wait_recv()
    finish(half, product(half, 0, GROUPS))
    last = GROUPS - 1
    near_part = [product(k, 0, last) for k in range(1, half)]
    q_forward(last)
    for k in range(1, half):
        for g in range(last):
            ref = q_all.at[half + k, :, cols_of(g)]
            remote(ref, ref, q_send, q_far.at[k, g], rep=mate).wait_recv()
    far_part = [product(half + k, 0, last) for k in range(1, half)]
    for k in range(1, half):
        finish(k, near_part[k - 1] + product(k, last, GROUPS))
    for k in range(1, half):
        ref = q_all.at[half + k, :, cols_of(last)]
        remote(ref, ref, q_send, q_far.at[k, last], rep=mate).wait_recv()
        finish(half + k, far_part[k - 1] + product(half + k, last, GROUPS))

    for k in range(1, n_rep):
        remote(stat_all.at[rep], stat_all.at[rep], stat_sem.at[0], stat_sem.at[1],
               rep=(rep + k) % n_rep).start()
    others = pos_all.at[0:n_rep - 1]
    remote(others, others, pos_sem.at[0], pos_sem.at[1], rep=mate).wait()
    others = gain_all.at[0:n_fsdp - 1]
    remote(others, others, gain_sem.at[0], gain_sem.at[1], fsdp=p_mate).wait()
    remote(q_all.at[0:n_rep - 1], q_all.at[0:n_rep - 1], q_send, q_mate, rep=mate).wait_send()
    remote(p_all.at[0:n_fsdp - 1, 0:pas], p_all.at[0:n_fsdp - 1, 0:pas], p_send, p_far,
           fsdp=p_mate).wait_send()
    remote(a_all.at[1:n_fsdp], a_all.at[1:n_fsdp], a_sem.at[0], a_sem.at[1], fsdp=p_mate).wait()
    stats = stat_all.at[0:n_rep - 1]
    remote(stats, stats, stat_sem.at[0], stat_sem.at[1], rep=mate).wait()

    loss_part = jnp.zeros((1, 1), F32)
    weights = []
    for i, block in enumerate(order):
        tops = [stat_all[r, block, 0:1, 0:qry] for r in range(n_rep)]
        top = functools.reduce(jnp.maximum, tops)
        total = sum(stat_all[r, block, 1:2, 0:qry] * jnp.exp(tops[r] - top) for r in range(n_rep))
        log_total = top + jnp.log(total)
        s = scores[i]
        match = (pass_ids == pos_all[block]) & valid
        weights.append(jnp.exp(s - log_total) - jnp.where(match, 1.0, 0.0))
        hit = jnp.sum(jnp.where(match, s, 0.0), axis=0, keepdims=True)
        loss_part = loss_part - jnp.sum(hit, axis=1, keepdims=True)
        if i == 0:
            loss_part = loss_part + jnp.sum(log_total, axis=1, keepdims=True)
    weights = jnp.concatenate(weights, axis=1).astype(BF16)

    tile = min(1024, dim)
    for c in range(dim // tile):
        cols = slice(c * tile, (c + 1) * tile)
        grad = jnp.dot(weights, q_all[:, :, cols].reshape(n_rep * qry, tile),
                       preferred_element_type=F32) * score_scale
        grad_own[:, cols] = grad[0:p_half * PAD]
        for j in range(n_fsdp):
            top_own[j, :, cols] = grad[j * PAD:j * PAD + 1]
        for k in range(p_half):
            near_send[k, :, cols] = grad[(p_half + k) * PAD:(p_half + k + 1) * PAD].astype(BF16)

    passing = [turned(p_half - k)
               for k in sorted(range(1, p_half), key=lambda k: abs(2 * k - p_half))] + [0]

    def near_copy(k):
        return remote(near_send.at[k, 0:pas], near_recv.at[k, 0:pas], near_sent, near_got.at[k],
                      fsdp=p_mate)

    for k in passing[:-2]:
        near_copy(k).start()

    gain_term = jnp.zeros((1, dim), F32)
    for j in range(n_fsdp):
        row = p_all[j, 0:1, :].astype(F32)
        own = top_own[j]
        inner = jnp.sum(row * own, axis=-1, keepdims=True)
        gain_term = gain_term + a_all[j] * (own - row * inner)
    for f in range(n_fsdp):
        share_send[f, :, 0:part] = gain_term[:, f * part:(f + 1) * part]
        share_send[f, :, part:] = jnp.broadcast_to(loss_part, (1, LANES))
    for j in range(1, n_fsdp):
        remote(share_send.at[who(j)], share_recv.at[mirror(j)], share_sem.at[0], share_sem.at[1],
               fsdp=who(j)).start()
    near_copy(passing[-2]).start()
    cut = dim // 2
    for j in range(1, n_fsdp):
        own = top_own[j]
        top_send[j] = jnp.concatenate([own[:, :cut], own[:, cut:]], axis=0).astype(BF16)
        remote(top_send.at[j], top_recv.at[mirror(j)], top_sem.at[0], top_sem.at[1],
               fsdp=who(j)).start()
    near_copy(0).start()

    def pass_on(k):
        near_copy(k).wait_recv()
        rows = pl.ds(pl.multiple_of(k * PAD, PAD), PAD)
        far_send[k] = (grad_own[rows, :] + near_recv[k].astype(F32)).astype(BF16)
        remote(far_send.at[k, 0:pas], far_recv.at[p_half - k, 0:pas], far_sem.at[0],
               far_sem.at[1], fsdp=(fsdp + 2 * k) % n_fsdp).start()

    for k in passing[:-1]:
        pass_on(k)

    remote(share_recv.at[1:n_fsdp], share_recv.at[1:n_fsdp], share_sem.at[0], share_sem.at[1],
           fsdp=p_mate).wait()
    share_recv[0] = share_send[fsdp]
    total_all[rep] = sum(share_recv[f] for f in range(n_fsdp))
    for k in range(1, n_rep):
        remote(total_all.at[rep], total_all.at[rep], total_sem.at[0], total_sem.at[1],
               rep=(rep + k) % n_rep).start()

    remote(top_recv.at[1:n_fsdp], top_recv.at[1:n_fsdp], top_sem.at[0], top_sem.at[1],
           fsdp=p_mate).wait()
    own = top_own[0]
    top_grad = jnp.concatenate([own[:, :cut], own[:, cut:]], axis=0)
    for j in range(1, n_fsdp):
        top_grad = top_grad + top_recv[j].astype(F32)
    top_grad = jnp.concatenate([top_grad[0:1], top_grad[1:2]], axis=1)
    row = p_dir[0:1, :]
    top_grad = (top_grad - row * jnp.sum(row * top_grad, axis=-1, keepdims=True)) * p_inv[0:1]
    slope = top_grad / length
    for f in range(n_fsdp):
        scaled = gain_all[f] * slope[:, f * part:(f + 1) * part]
        wide[:, f * part:(f + 1) * part] = jnp.broadcast_to(scaled, (16, part))

    def last_pass(i, _):
        rows = pl.ds(pl.multiple_of(i * 16, 16), 16)
        inner = jnp.sum(h_in[rows, :].astype(F32) * wide[...], axis=-1, keepdims=True)
        inv = row_inv[rows, 0:1]
        coef = inner * (inv * inv * inv) / dim
        h_out[rows, :] = (wide[...] * inv - h_in[rows, :].astype(F32) * coef).astype(BF16)
        return 0

    lax.fori_loop(0, length // 16, last_pass, 0, unroll=2)
    near_copy(0).wait_recv()
    unit_grad = grad_own[0:PAD, :] + near_recv[0].astype(F32)

    totals = total_all.at[0:n_rep - 1]
    remote(totals, totals, total_sem.at[0], total_sem.at[1], rep=mate).wait()
    total = sum(total_all[r] for r in range(n_rep))
    gg_out[...] = total[:, 0:part]
    loss_out[...] = total[:, part:] / (qry * n_rep * n_fsdp)
    remote(near_send.at[:, 0:pas], near_recv.at[:, 0:pas], near_sent, near_got.at[0],
           fsdp=p_mate).wait_send()

    sums = far_recv.at[1:p_half, 0:pas]
    remote(sums, sums, far_sem.at[0], far_sem.at[1], fsdp=p_mate).wait()
    for k in range(1, p_half):
        unit_grad = unit_grad + far_recv[k].astype(F32)
    unit_grad = unit_grad[0:pas]
    rows_dir = p_dir[...]
    pg_out[...] = (
        unit_grad - rows_dir * jnp.sum(rows_dir * unit_grad, axis=-1, keepdims=True)) * p_inv
    pg_out[0:1, :] = top_grad


def write_out(*refs):
    count = (len(refs) - 1) // 2
    sems = refs[-1]
    copies = [pltpu.make_async_copy(refs[i], refs[count + i], sems.at[i]) for i in range(count)]
    for copy in copies:
        copy.start()
    for copy in copies:
        copy.wait()


def per_device(query_cache, passage_cache, positives, norm_gain, hidden_states):
    n_rep, n_fsdp = lax.axis_size("rep"), lax.axis_size("fsdp")
    qry, dim = query_cache.shape
    pas = passage_cache.shape[0]
    length = hidden_states.shape[0]
    part = dim // n_fsdp
    half, p_half = n_rep // 2, n_fsdp // 2
    vmem = pl.BlockSpec(memory_space=pltpu.VMEM)
    hbm = pl.BlockSpec(memory_space=pltpu.HBM)
    dma = pltpu.SemaphoreType.DMA
    results = pl.pallas_call(
        functools.partial(kernel, n_rep, n_fsdp),
        name="step",
        out_shape=(
            pltpu.VMEM((1, LANES), F32),
            pltpu.VMEM((pas, dim), F32),
            pltpu.VMEM((length, dim), BF16),
            pltpu.VMEM((1, part), F32),
        ),
        in_specs=[hbm] * 5,
        out_specs=(vmem, vmem, vmem, vmem),
        scratch_shapes=[
            pltpu.VMEM((qry, dim), BF16),
            pltpu.VMEM((pas, dim), BF16),
            pltpu.VMEM((length, dim), BF16),
            pltpu.VMEM((n_rep, qry, dim), BF16),
            pltpu.VMEM((n_fsdp, PAD, dim), BF16),
            pltpu.VMEM((pas, dim), F32),
            pltpu.VMEM((n_rep, 1, qry), jnp.int32),
            pltpu.VMEM((n_fsdp, 1, part), F32),
            pltpu.VMEM((n_rep, n_fsdp * PAD, qry), F32),
            pltpu.VMEM((n_rep, n_rep, 2, LANES), F32),
            pltpu.VMEM((n_fsdp, 1, dim), F32),
            pltpu.VMEM((n_fsdp, 1, dim), F32),
            pltpu.VMEM((n_fsdp, 2, dim // 2), BF16),
            pltpu.VMEM((n_fsdp, 2, dim // 2), BF16),
            pltpu.VMEM((p_half, PAD, dim), BF16),
            pltpu.VMEM((p_half, PAD, dim), BF16),
            pltpu.VMEM((p_half, PAD, dim), BF16),
            pltpu.VMEM((p_half, PAD, dim), BF16),
            pltpu.VMEM((p_half * PAD, dim), F32),
            pltpu.VMEM((n_fsdp, 1, part + LANES), F32),
            pltpu.VMEM((n_fsdp, 1, part + LANES), F32),
            pltpu.VMEM((n_rep, 1, part + LANES), F32),
            pltpu.VMEM((8, dim), F32),
            pltpu.VMEM((length, LANES), F32),
            pltpu.VMEM((16, dim), F32),
            dma((5,)),
            dma, dma((half, GROUPS)), dma, dma((half, GROUPS)),
            dma, dma((p_half,)), dma,
            dma((2,)), dma((2,)), dma((2,)), dma((2,)), dma((2,)), dma((2,)), dma((2,)),
            dma, dma((p_half,)), dma((2,)),
        ],
        compiler_params=pltpu.CompilerParams(
            collective_id=0, has_side_effects=True, vmem_limit_bytes=40 << 20),
    )(*[pltpu.with_memory_space_constraint(array, pltpu.HBM) for array in (
        query_cache, passage_cache, positives.reshape(1, qry), norm_gain.reshape(1, part),
        hidden_states)])
    loss, passage_grad, hidden_grad, gain_grad = pl.pallas_call(
        write_out,
        name="write_out",
        out_shape=tuple(pltpu.HBM(r.shape, r.dtype) for r in results),
        in_specs=[vmem] * 4,
        out_specs=(hbm,) * 4,
        scratch_shapes=[dma((4,))],
    )(*[pltpu.with_memory_space_constraint(r, pltpu.VMEM) for r in results])
    return loss[0, 0], passage_grad, hidden_grad, gain_grad.reshape(part)


def solution(mesh):
    return jax.shard_map(
        per_device,
        mesh=mesh,
        in_specs=(
            P(("rep", "fsdp"), None),
            P(("rep", "fsdp"), None),
            P(("rep", "fsdp")),
            P("fsdp"),
            P(("rep", "fsdp"), None),
        ),
        out_specs=(P(), P(("rep", "fsdp"), None), P(("rep", "fsdp"), None), P("fsdp")),
        check_vma=False,
    )
```

```python
import functools

import jax
import jax.numpy as jnp
from jax import lax
from jax.experimental import pallas as pl
from jax.experimental.pallas import tpu as pltpu
from jax.sharding import PartitionSpec as P

score_scale = 256.0
PAD = 8
LANES = 128
GROUPS = 4
F32 = jnp.float32
BF16 = jnp.bfloat16


def remote(src, dst, send_sem, recv_sem, **where):
    return pltpu.make_async_remote_copy(
        src_ref=src,
        dst_ref=dst,
        send_sem=send_sem,
        recv_sem=recv_sem,
        device_id=where,
        device_id_type=pl.DeviceIdType.MESH,
    )


def kernel(
    n_rep, n_fsdp, q_hbm, p_hbm, pos_ref, gain_ref, h_hbm,
    loss_out, pg_out, h_out, gg_out,
    q_in, p_in, h_in, q_all, p_all, p_dir, pos_all, gain_all, scores, stat_all,
    a_all, top_own, top_send, top_recv, near_send, near_recv, far_send, far_recv, grad_own,
    share_send, share_recv, total_all, col_acc, row_inv, row_coef, wide,
    in_sem, q_sem, q_send, q_near, q_mate, q_far, p_send, p_near, p_far, pos_sem, gain_sem, a_sem,
    stat_sem, top_sem, share_sem, total_sem, near_sent, near_got, far_sem,
):
    rep, fsdp = lax.axis_index("rep"), lax.axis_index("fsdp")
    qry, dim = q_in.shape
    pas = p_in.shape[0]
    length = h_in.shape[0]
    rest = pas - 2
    half = n_rep // 2
    p_half = n_fsdp // 2
    part = dim // n_fsdp
    width = dim // GROUPS
    mate = rep + 1 - 2 * (rep % 2)
    p_mate = fsdp + 1 - 2 * (fsdp % 2)
    odd = (fsdp // 2) % 2

    def turned(k):
        return odd * (p_half - k) + (1 - odd) * k

    barrier = pltpu.get_barrier_semaphore()
    direct = [{"rep": mate}, {"fsdp": p_mate}]
    direct += [{"rep": (rep + 2 * k) % n_rep} for k in range(1, half)]
    direct += [{"fsdp": (fsdp + 2 * k) % n_fsdp} for k in range(1, p_half)]
    for where in direct:
        pl.semaphore_signal(barrier, inc=1, device_id=where, device_id_type=pl.DeviceIdType.MESH)

    q_loads = [
        pltpu.make_async_copy(q_hbm.at[c * 16:(c + 1) * 16], q_in.at[c * 16:(c + 1) * 16], q_sem.at[c])
        for c in range(qry // 16)
    ]
    loads = [
        pltpu.make_async_copy(p_hbm, p_in, in_sem.at[0]),
        pltpu.make_async_copy(pos_ref, pos_all.at[rep], in_sem.at[1]),
        pltpu.make_async_copy(gain_ref, gain_all.at[fsdp], in_sem.at[2]),
        pltpu.make_async_copy(h_hbm, h_in, in_sem.at[3]),
    ]
    for load in q_loads + loads[:3]:
        load.start()

    def who(j):
        return ((fsdp + 2 * j) if j < p_half else (p_mate + 2 * (j - p_half))) % n_fsdp

    def mirror(j):
        return (-j) % p_half if j < p_half else p_half + (-(j - p_half)) % p_half

    for c in range(qry // 16):
        q_loads[c].wait()
        rows = slice(c * 16, (c + 1) * 16)
        raw = q_in[rows, :].astype(F32)
        radius = jnp.sqrt(jnp.sum(raw * raw, axis=-1, keepdims=True) + 1e-06)
        q_all[0, rows, :] = (q_in[rows, :].astype(F32) * (1.0 / radius)).astype(BF16)

    loads[3].start()
    pl.semaphore_wait(barrier, len(direct))

    def cols_of(g):
        return slice(g * width, (g + 1) * width)

    def p_block(j):
        return p_all.at[j, 0:pas]

    for g in range(GROUPS):
        for k in range(1, half):
            remote(q_all.at[0, :, cols_of(g)], q_all.at[half - k, :, cols_of(g)], q_send,
                   q_near.at[half - k - 1, g], rep=(rep + 2 * k) % n_rep).start()
    remote(q_all.at[0], q_all.at[half], q_send, q_mate, rep=mate).start()

    loads[0].wait()
    wide_p = p_in[...].astype(F32)
    p_radius = jnp.sqrt(jnp.sum(wide_p * wide_p, axis=-1, keepdims=True) + 1e-06)
    p_inv = 1.0 / p_radius
    p_dir[...] = wide_p * p_inv
    p_all[0] = jnp.concatenate(
        [p_dir[2:pas], p_dir[0:2], jnp.zeros((PAD - pas, dim), F32)], axis=0).astype(BF16)
    for k in range(1, p_half):
        k = turned(k)
        remote(p_block(0), p_block(p_half - k), p_send, p_near.at[p_half - k - 1],
               fsdp=(fsdp + 2 * k) % n_fsdp).start()
    remote(p_block(0), p_block(p_half), p_send, p_far, fsdp=p_mate).start()

    loads[3].wait()
    col_acc[...] = jnp.zeros_like(col_acc)

    def first_pass(i, _):
        rows = pl.ds(pl.multiple_of(i * 16, 16), 16)
        x = h_in[rows, :].astype(F32)
        inv = 1.0 / jnp.sqrt(jnp.sum(x * x, axis=-1, keepdims=True) / dim + 1e-05)
        row_inv[rows, :] = jnp.broadcast_to(inv, (16, LANES))
        y = h_in[rows, :].astype(F32) * inv
        col_acc[...] += y[:8] + y[8:]
        return 0

    lax.fori_loop(0, length // 16, first_pass, 0)
    colsum = jnp.sum(col_acc[...], axis=0, keepdims=True)
    a_all[0] = colsum * (p_inv[0:1] / length)

    def q_forward(g):
        for k in range(1, half):
            ref = q_all.at[k, :, cols_of(g)]
            remote(ref, ref, q_send, q_near.at[k - 1, g], rep=mate).wait_recv()
            remote(ref, q_all.at[half + k, :, cols_of(g)], q_send, q_far.at[k - 1, g // (GROUPS - 1)],
                   rep=mate).start()

    def p_forward(k):
        remote(p_block(k), p_block(k), p_send, p_near.at[k - 1], fsdp=p_mate).wait_recv()
        remote(p_block(k), p_block(p_half + k), p_send, p_far, fsdp=p_mate).start()

    for k in range(1, p_half):
        p_forward(turned(k))
    q_forward(0)
    loads[1].wait()
    loads[2].wait()
    for k in range(1, n_rep):
        remote(pos_all.at[rep], pos_all.at[rep], pos_sem.at[0], pos_sem.at[1],
               rep=(rep + k) % n_rep).start()
    for k in range(1, n_fsdp):
        remote(gain_all.at[fsdp], gain_all.at[fsdp], gain_sem.at[0], gain_sem.at[1],
               fsdp=(fsdp + k) % n_fsdp).start()
    for j in range(1, n_fsdp):
        remote(a_all.at[0], a_all.at[mirror(j)], a_sem.at[0], a_sem.at[1], fsdp=who(j)).start()
    for g in range(1, GROUPS - 1):
        q_forward(g)
    remote(p_all.at[0:p_half, 0:pas], p_all.at[p_half:n_fsdp, 0:pas], p_send, p_far,
           fsdp=p_mate).wait_recv()

    rows_all = n_fsdp * PAD
    slot = lax.broadcasted_iota(jnp.int32, (rows_all, qry), 0)
    lane = slot % PAD
    valid = lane < pas
    index = slot // PAD
    source = jnp.where(index < p_half, fsdp + 2 * index, p_mate + 2 * (index - p_half))
    source = jnp.where(source >= n_fsdp, source - n_fsdp, source)
    pass_ids = (rep * n_fsdp + source) * pas + jnp.where(lane < rest, lane + 2, lane - rest)

    order = [(rep + 2 * k) % n_rep for k in range(half)] + [(mate + 2 * k) % n_rep for k in range(half)]

    def product(i, g0, g1):
        cols = slice(g0 * width, g1 * width)
        return lax.dot_general(p_all[:, :, cols].reshape(rows_all, (g1 - g0) * width), q_all[i, :, cols],
                               (((1,), (1,)), ((), ())), preferred_element_type=F32)

    def finish(i, s):
        s = jnp.where(valid, s * score_scale, -1e30)
        scores[i] = s
        top = jnp.max(s, axis=0, keepdims=True)
        stat_all[rep, order[i], 0:1, 0:qry] = top
        stat_all[rep, order[i], 1:2, 0:qry] = jnp.sum(jnp.exp(s - top), axis=0, keepdims=True)

    stat_all[rep] = jnp.zeros(stat_all.shape[1:], F32)
    finish(0, product(0, 0, GROUPS))
    remote(q_all.at[0], q_all.at[half], q_send, q_mate, rep=mate).wait_recv()
    finish(half, product(half, 0, GROUPS))
    last = GROUPS - 1
    near_part = [product(k, 0, last) for k in range(1, half)]
    q_forward(last)
    for k in range(1, half):
        ref = q_all.at[half + k, :, 0:last * width]
        remote(ref, ref, q_send, q_far.at[k - 1, 0], rep=mate).wait_recv()
    far_part = [product(half + k, 0, last) for k in range(1, half)]
    for k in range(1, half):
        finish(k, near_part[k - 1] + product(k, last, GROUPS))
    for k in range(1, half):
        ref = q_all.at[half + k, :, cols_of(last)]
        remote(ref, ref, q_send, q_far.at[k - 1, 1], rep=mate).wait_recv()
        finish(half + k, far_part[k - 1] + product(half + k, last, GROUPS))

    for k in range(1, n_rep):
        remote(stat_all.at[rep], stat_all.at[rep], stat_sem.at[0], stat_sem.at[1],
               rep=(rep + k) % n_rep).start()
    others = pos_all.at[0:n_rep - 1]
    remote(others, others, pos_sem.at[0], pos_sem.at[1], rep=mate).wait()
    others = gain_all.at[0:n_fsdp - 1]
    remote(others, others, gain_sem.at[0], gain_sem.at[1], fsdp=p_mate).wait()
    remote(q_all.at[0:n_rep - 1], q_all.at[0:n_rep - 1], q_send, q_mate, rep=mate).wait_send()
    remote(p_all.at[0:n_fsdp - 1, 0:pas], p_all.at[0:n_fsdp - 1, 0:pas], p_send, p_far,
           fsdp=p_mate).wait_send()
    remote(a_all.at[1:n_fsdp], a_all.at[1:n_fsdp], a_sem.at[0], a_sem.at[1], fsdp=p_mate).wait()
    stats = stat_all.at[0:n_rep - 1]
    remote(stats, stats, stat_sem.at[0], stat_sem.at[1], rep=mate).wait()

    loss_part = jnp.zeros((1, 1), F32)
    weights = []
    for i, block in enumerate(order):
        tops = [stat_all[r, block, 0:1, 0:qry] for r in range(n_rep)]
        top = functools.reduce(jnp.maximum, tops)
        total = sum(stat_all[r, block, 1:2, 0:qry] * jnp.exp(tops[r] - top) for r in range(n_rep))
        log_total = top + jnp.log(total)
        s = scores[i]
        match = (pass_ids == pos_all[block]) & valid
        weights.append(jnp.exp(s - log_total) - jnp.where(match, 1.0, 0.0))
        hit = jnp.sum(jnp.where(match, s, 0.0), axis=0, keepdims=True)
        loss_part = loss_part - jnp.sum(hit, axis=1, keepdims=True)
        if i == 0:
            loss_part = loss_part + jnp.sum(log_total, axis=1, keepdims=True)
    weights = jnp.concatenate(weights, axis=1).astype(BF16)

    tile = min(1024, dim)
    for c in range(dim // tile):
        cols = slice(c * tile, (c + 1) * tile)
        grad = jnp.dot(weights, q_all[:, :, cols].reshape(n_rep * qry, tile),
                       preferred_element_type=F32) * score_scale
        grad_own[:, cols] = grad[0:p_half * PAD]
        for j in range(n_fsdp):
            for r in range(2):
                at = j * PAD + rest + r
                top_own[r, j, :, cols] = grad[at:at + 1]
        for k in range(p_half):
            near_send[k, :, cols] = grad[(p_half + k) * PAD:(p_half + k + 1) * PAD].astype(BF16)

    passing = [turned(p_half - k)
               for k in sorted(range(1, p_half), key=lambda k: abs(2 * k - p_half))] + [0]

    def near_copy(k):
        return remote(near_send.at[k, 0:rest], near_recv.at[k, 0:rest], near_sent, near_got.at[k],
                      fsdp=p_mate)

    for k in passing[:-1]:
        near_copy(k).start()

    gain_term = jnp.zeros((1, dim), F32)
    for j in range(n_fsdp):
        row = p_all[j, rest:rest + 1, :].astype(F32)
        own = top_own[0, j]
        inner = jnp.sum(row * own, axis=-1, keepdims=True)
        gain_term = gain_term + a_all[j] * (own - row * inner)
    for f in range(n_fsdp):
        share_send[f, :, 0:part] = gain_term[:, f * part:(f + 1) * part]
        share_send[f, :, part:] = jnp.broadcast_to(loss_part, (1, LANES))
    for k in range(half):
        for j in range(n_fsdp):
            if k or j:
                remote(share_send.at[who(j)], share_recv.at[(-k) % half * n_fsdp + mirror(j)],
                       share_sem.at[0], share_sem.at[1],
                       rep=(rep + 2 * k) % n_rep, fsdp=who(j)).start()
    cut = dim // 2

    def folded(own):
        return jnp.concatenate([own[:, :cut], own[:, cut:]], axis=0)

    def flat(pair):
        return jnp.concatenate([pair[0:1], pair[1:2]], axis=1)

    for r in range(2):
        for j in range(1, n_fsdp):
            top_send[r, j] = folded(top_own[r, j]).astype(BF16)
            remote(top_send.at[r, j], top_recv.at[r, mirror(j)], top_sem.at[r], top_sem.at[2 + r],
                   fsdp=who(j)).start()
    near_copy(0).start()

    for k in passing[:-1]:
        near_copy(k).wait_recv()
        rows = pl.ds(pl.multiple_of(k * PAD, PAD), PAD)
        far_send[k] = (grad_own[rows, :] + near_recv[k].astype(F32)).astype(BF16)
        remote(far_send.at[k, 0:rest], far_recv.at[p_half - k, 0:rest], far_sem.at[0],
               far_sem.at[1], fsdp=(fsdp + 2 * k) % n_fsdp).start()

    def row_sum(r):
        sums = top_recv.at[r, 1:n_fsdp]
        remote(sums, sums, top_sem.at[r], top_sem.at[2 + r], fsdp=p_mate).wait()
        total = folded(top_own[r, 0])
        for j in range(1, n_fsdp):
            total = total + top_recv[r, j].astype(F32)
        return flat(total)

    def final(total, rows):
        row = p_dir[rows, :]
        return (total - row * jnp.sum(row * total, axis=-1, keepdims=True)) * p_inv[rows]

    shares = share_recv.at[1:half * n_fsdp]
    remote(shares, shares, share_sem.at[0], share_sem.at[1], fsdp=p_mate).wait()
    total = share_send[fsdp]
    for f in range(1, half * n_fsdp):
        total = total + share_recv[f]
    total_all[0] = total
    total_copy = remote(total_all.at[0], total_all.at[1], total_sem.at[0], total_sem.at[1], rep=mate)
    total_copy.start()

    top_grad = final(row_sum(0), slice(0, 1))
    pg_out[0:1, :] = top_grad
    slope = top_grad / length
    for f in range(n_fsdp):
        scaled = gain_all[f] * slope[:, f * part:(f + 1) * part]
        wide[:, f * part:(f + 1) * part] = jnp.broadcast_to(scaled, (16, part))

    def inner_pass(i, _):
        rows = pl.ds(pl.multiple_of(i * 16, 16), 16)
        acc = h_in[rows, 0:LANES].astype(F32) * wide[:, 0:LANES]
        for l in range(1, dim // LANES):
            cols = slice(l * LANES, (l + 1) * LANES)
            acc = acc + h_in[rows, cols].astype(F32) * wide[:, cols]
        row_coef[rows, :] = acc
        return 0

    lax.fori_loop(0, length // 16, inner_pass, 0, unroll=4)
    inv = row_inv[...]
    inner = jnp.sum(row_coef[...], axis=-1, keepdims=True)
    row_coef[...] = inner * (inv * inv * inv) / dim

    def last_pass(i, _):
        rows = pl.ds(pl.multiple_of(i * 16, 16), 16)
        inv = row_inv[rows, :]
        coef = row_coef[rows, :]
        for l in range(dim // LANES):
            cols = slice(l * LANES, (l + 1) * LANES)
            h_out[rows, cols] = (wide[:, cols] * inv - h_in[rows, cols].astype(F32) * coef).astype(BF16)
        return 0

    lax.fori_loop(0, length // 16, last_pass, 0, unroll=2)
    pg_out[1:2, :] = final(row_sum(1), slice(1, 2))

    near_copy(0).wait_recv()
    unit_grad = grad_own[0:PAD, :] + near_recv[0].astype(F32)

    total_copy.wait()
    total = total_all[0] + total_all[1]
    gg_out[...] = total[:, 0:part]
    loss_out[...] = total[:, part:] / (qry * n_rep * n_fsdp)
    remote(near_send.at[:, 0:rest], near_recv.at[:, 0:rest], near_sent, near_got.at[0],
           fsdp=p_mate).wait_send()

    sums = far_recv.at[1:p_half, 0:rest]
    remote(sums, sums, far_sem.at[0], far_sem.at[1], fsdp=p_mate).wait()
    for k in range(1, p_half):
        unit_grad = unit_grad + far_recv[k].astype(F32)
    pg_out[2:pas, :] = final(unit_grad[0:rest], slice(2, pas))


def write_out(*refs):
    count = (len(refs) - 1) // 2
    sems = refs[-1]
    copies = [pltpu.make_async_copy(refs[i], refs[count + i], sems.at[i]) for i in range(count)]
    for copy in copies:
        copy.start()
    for copy in copies:
        copy.wait()


def per_device(query_cache, passage_cache, positives, norm_gain, hidden_states):
    n_rep, n_fsdp = lax.axis_size("rep"), lax.axis_size("fsdp")
    qry, dim = query_cache.shape
    pas = passage_cache.shape[0]
    length = hidden_states.shape[0]
    part = dim // n_fsdp
    half, p_half = n_rep // 2, n_fsdp // 2
    vmem = pl.BlockSpec(memory_space=pltpu.VMEM)
    hbm = pl.BlockSpec(memory_space=pltpu.HBM)
    dma = pltpu.SemaphoreType.DMA
    results = pl.pallas_call(
        functools.partial(kernel, n_rep, n_fsdp),
        name="step",
        out_shape=(
            pltpu.VMEM((1, LANES), F32),
            pltpu.VMEM((pas, dim), F32),
            pltpu.VMEM((length, dim), BF16),
            pltpu.VMEM((1, part), F32),
        ),
        in_specs=[hbm] * 5,
        out_specs=(vmem, vmem, vmem, vmem),
        scratch_shapes=[
            pltpu.VMEM((qry, dim), BF16),
            pltpu.VMEM((pas, dim), BF16),
            pltpu.VMEM((length, dim), BF16),
            pltpu.VMEM((n_rep, qry, dim), BF16),
            pltpu.VMEM((n_fsdp, PAD, dim), BF16),
            pltpu.VMEM((pas, dim), F32),
            pltpu.VMEM((n_rep, 1, qry), jnp.int32),
            pltpu.VMEM((n_fsdp, 1, part), F32),
            pltpu.VMEM((n_rep, n_fsdp * PAD, qry), F32),
            pltpu.VMEM((n_rep, n_rep, 2, LANES), F32),
            pltpu.VMEM((n_fsdp, 1, dim), F32),
            pltpu.VMEM((2, n_fsdp, 1, dim), F32),
            pltpu.VMEM((2, n_fsdp, 2, dim // 2), BF16),
            pltpu.VMEM((2, n_fsdp, 2, dim // 2), BF16),
            pltpu.VMEM((p_half, PAD, dim), BF16),
            pltpu.VMEM((p_half, PAD, dim), BF16),
            pltpu.VMEM((p_half, PAD, dim), BF16),
            pltpu.VMEM((p_half, PAD, dim), BF16),
            pltpu.VMEM((p_half * PAD, dim), F32),
            pltpu.VMEM((n_fsdp, 1, part + LANES), F32),
            pltpu.VMEM((half * n_fsdp, 1, part + LANES), F32),
            pltpu.VMEM((2, 1, part + LANES), F32),
            pltpu.VMEM((8, dim), F32),
            pltpu.VMEM((length, LANES), F32),
            pltpu.VMEM((length, LANES), F32),
            pltpu.VMEM((16, dim), F32),
            dma((4,)), dma((qry // 16,)),
            dma, dma((half - 1, GROUPS)), dma, dma((half - 1, 2)),
            dma, dma((p_half - 1,)), dma,
            dma((2,)), dma((2,)), dma((2,)), dma((2,)), dma((4,)), dma((2,)), dma((2,)),
            dma, dma((p_half,)), dma((2,)),
        ],
        compiler_params=pltpu.CompilerParams(
            collective_id=0, has_side_effects=True, vmem_limit_bytes=40 << 20),
    )(*[pltpu.with_memory_space_constraint(array, pltpu.HBM) for array in (
        query_cache, passage_cache, positives.reshape(1, qry), norm_gain.reshape(1, part),
        hidden_states)])
    loss, passage_grad, hidden_grad, gain_grad = pl.pallas_call(
        write_out,
        name="write_out",
        out_shape=tuple(pltpu.HBM(r.shape, r.dtype) for r in results),
        in_specs=[vmem] * 4,
        out_specs=(hbm,) * 4,
        scratch_shapes=[dma((4,))],
    )(*[pltpu.with_memory_space_constraint(r, pltpu.VMEM) for r in results])
    return loss[0, 0], passage_grad, hidden_grad, gain_grad.reshape(part)


def solution(mesh):
    return jax.shard_map(
        per_device,
        mesh=mesh,
        in_specs=(
            P(("rep", "fsdp"), None),
            P(("rep", "fsdp"), None),
            P(("rep", "fsdp")),
            P("fsdp"),
            P(("rep", "fsdp"), None),
        ),
        out_specs=(P(), P(("rep", "fsdp"), None), P(("rep", "fsdp"), None), P("fsdp")),
        check_vma=False,
    )
```

```python
import functools

import jax
import jax.numpy as jnp
from jax import lax
from jax.experimental import pallas as pl
from jax.experimental.pallas import tpu as pltpu
from jax.sharding import PartitionSpec as P

score_scale = 256.0
PAD = 8
LANES = 128
GROUPS = 4
F32 = jnp.float32
BF16 = jnp.bfloat16


def remote(src, dst, send_sem, recv_sem, **where):
    return pltpu.make_async_remote_copy(
        src_ref=src,
        dst_ref=dst,
        send_sem=send_sem,
        recv_sem=recv_sem,
        device_id=where,
        device_id_type=pl.DeviceIdType.MESH,
    )


def kernel(
    n_rep, n_fsdp, q_hbm, p_hbm, pos_ref, gain_ref, h_hbm,
    loss_out, pg_out, h_out, gg_out,
    q_in, p_in, h_in, q_all, p_all, p_dir, pos_all, gain_all, scores, score_send, w_all, stat_all,
    a_all, top_own, top_send, top_recv, near_send, near_recv, far_send, far_recv, grad_own,
    share_send, share_recv, total_all, col_acc, row_inv, row_coef, wide,
    in_sem, q_sem, q_send, q_near, q_mate, q_far, p_send, p_near, p_far, p_core, pos_sem, gain_sem, a_sem,
    stat_sem, score_sem, top_sem, share_sem, total_sem, near_sent, near_got, far_sem,
):
    rep, fsdp = lax.axis_index("rep"), lax.axis_index("fsdp")
    qry, dim = q_in.shape
    pas = p_in.shape[0]
    length = h_in.shape[0]
    rest = pas - 2
    half = n_rep // 2
    p_half = n_fsdp // 2
    part = dim // n_fsdp
    width = dim // GROUPS
    mate = rep + 1 - 2 * (rep % 2)
    p_mate = fsdp + 1 - 2 * (fsdp % 2)
    odd = (fsdp // 2) % 2

    def turned(k):
        return odd * (p_half - k) + (1 - odd) * k

    barrier = pltpu.get_barrier_semaphore()
    direct = [{"rep": mate}, {"fsdp": p_mate}]
    direct += [{"rep": (rep + 2 * k) % n_rep} for k in range(1, half)]
    direct += [{"fsdp": (fsdp + 2 * k) % n_fsdp} for k in range(1, p_half)]
    for where in direct:
        pl.semaphore_signal(barrier, inc=1, device_id=where, device_id_type=pl.DeviceIdType.MESH)

    q_loads = [
        pltpu.make_async_copy(q_hbm.at[c * 16:(c + 1) * 16], q_in.at[c * 16:(c + 1) * 16], q_sem.at[c])
        for c in range(qry // 16)
    ]
    loads = [
        pltpu.make_async_copy(p_hbm, p_in, in_sem.at[0]),
        pltpu.make_async_copy(pos_ref, pos_all.at[rep], in_sem.at[1]),
        pltpu.make_async_copy(gain_ref, gain_all.at[fsdp], in_sem.at[2]),
        pltpu.make_async_copy(h_hbm, h_in, in_sem.at[3]),
    ]
    for load in q_loads + loads[:3]:
        load.start()

    def who(j):
        return ((fsdp + 2 * j) if j < p_half else (p_mate + 2 * (j - p_half))) % n_fsdp

    def mirror(j):
        return (-j) % p_half if j < p_half else p_half + (-(j - p_half)) % p_half

    for c in range(qry // 16):
        q_loads[c].wait()
        rows = slice(c * 16, (c + 1) * 16)
        raw = q_in[rows, :].astype(F32)
        radius = jnp.sqrt(jnp.sum(raw * raw, axis=-1, keepdims=True) + 1e-06)
        q_all[0, rows, :] = (q_in[rows, :].astype(F32) * (1.0 / radius)).astype(BF16)

    loads[3].start()
    pl.semaphore_wait(barrier, len(direct))

    def cols_of(g):
        return slice(g * width, (g + 1) * width)

    def p_block(j):
        return p_all.at[j, 0:pas]

    for g in range(GROUPS):
        for k in range(1, half):
            remote(q_all.at[0, :, cols_of(g)], q_all.at[half - k, :, cols_of(g)], q_send,
                   q_near.at[half - k - 1, g], rep=(rep + 2 * k) % n_rep).start()
    remote(q_all.at[0], q_all.at[half], q_send, q_mate, rep=mate).start()

    loads[0].wait()
    wide_p = p_in[...].astype(F32)
    p_radius = jnp.sqrt(jnp.sum(wide_p * wide_p, axis=-1, keepdims=True) + 1e-06)
    p_inv = 1.0 / p_radius
    p_dir[...] = wide_p * p_inv
    p_all[0] = jnp.concatenate(
        [p_dir[2:pas], p_dir[0:2], jnp.zeros((PAD - pas, dim), F32)], axis=0).astype(BF16)
    for k in range(1, p_half):
        k = turned(k)
        remote(p_block(0), p_block(p_half - k), p_send, p_near.at[p_half - k - 1],
               fsdp=(fsdp + 2 * k) % n_fsdp).start()
    remote(p_block(0), p_block(p_half), p_send, p_far.at[0], fsdp=p_mate).start()

    def p_across(j):
        remote(p_block(j), p_block(n_fsdp + j), p_send, p_core, rep=mate).start()

    p_across(0)
    loads[3].wait()
    col_acc[...] = jnp.zeros_like(col_acc)

    def square_pass(i, _):
        rows = pl.ds(pl.multiple_of(i * 16, 16), 16)
        acc = None
        for l in range(dim // LANES):
            x = h_in[rows, l * LANES:(l + 1) * LANES].astype(F32)
            acc = x * x if acc is None else acc + x * x
        row_coef[rows, :] = acc
        return 0

    lax.fori_loop(0, length // 16, square_pass, 0, unroll=4)
    square = jnp.sum(row_coef[...], axis=-1, keepdims=True) / dim
    row_inv[...] = jnp.broadcast_to(1.0 / jnp.sqrt(square + 1e-05), row_inv.shape)

    def column_pass(i, _):
        rows = pl.ds(pl.multiple_of(i * 32, 32), 32)
        inv = row_inv[rows, :]
        for l in range(dim // LANES):
            cols = slice(l * LANES, (l + 1) * LANES)
            y = h_in[rows, cols].astype(F32) * inv
            col_acc[:, cols] += (y[:8] + y[8:16]) + (y[16:24] + y[24:])
        return 0

    lax.fori_loop(0, length // 32, column_pass, 0, unroll=2)
    colsum = jnp.sum(col_acc[...], axis=0, keepdims=True)
    a_all[0] = colsum * (p_inv[0:1] / length)

    def q_forward(g):
        for k in range(1, half):
            ref = q_all.at[k, :, cols_of(g)]
            remote(ref, ref, q_send, q_near.at[k - 1, g], rep=mate).wait_recv()
            remote(ref, q_all.at[half + k, :, cols_of(g)], q_send, q_far,
                   rep=mate).start()

    def p_forward(k):
        remote(p_block(k), p_block(k), p_send, p_near.at[k - 1], fsdp=p_mate).wait_recv()
        remote(p_block(k), p_block(p_half + k), p_send, p_far.at[k], fsdp=p_mate).start()
        p_across(k)

    def p_last(k):
        remote(p_block(k), p_block(p_half + k), p_send, p_far.at[k], fsdp=p_mate).wait_recv()
        p_across(p_half + k)

    for k in range(1, p_half):
        p_forward(turned(k))
    loads[1].wait()
    loads[2].wait()
    for k in range(1, n_fsdp):
        remote(gain_all.at[fsdp], gain_all.at[fsdp], gain_sem.at[0], gain_sem.at[1],
               fsdp=(fsdp + k) % n_fsdp).start()
    for j in range(1, n_fsdp):
        remote(a_all.at[0], a_all.at[mirror(j)], a_sem.at[0], a_sem.at[1], fsdp=who(j)).start()
    last = GROUPS - 1
    p_last(0)
    for g in range(last - 1):
        q_forward(g)
    for k in range(1, n_rep):
        remote(pos_all.at[rep], pos_all.at[rep], pos_sem.at[0], pos_sem.at[1],
               rep=(rep + k) % n_rep).start()
    for k in range(1, p_half):
        p_last(turned(k))

    rows_all = n_fsdp * PAD
    own_qry = half * qry
    slot = lax.broadcasted_iota(jnp.int32, (rows_all, own_qry), 0)
    lane = slot % PAD
    valid = lane < pas
    index = slot // PAD
    source = jnp.where(index < p_half, fsdp + 2 * index, p_mate + 2 * (index - p_half))
    source = jnp.where(source >= n_fsdp, source - n_fsdp, source)
    pass_ids = (rep * n_fsdp + source) * pas + jnp.where(lane < rest, lane + 2, lane - rest)

    order = [(rep + 2 * k) % n_rep for k in range(half)] + [(mate + 2 * k) % n_rep for k in range(half)]

    def product(first, end, g0, g1):
        cols = slice(g0 * width, g1 * width)
        rows = p_all[first:end, :, cols].reshape((end - first) * PAD, (g1 - g0) * width)
        return lax.dot_general(rows, q_all[0:half, :, cols].reshape(own_qry, (g1 - g0) * width),
                               (((1,), (1,)), ((), ())), preferred_element_type=F32)

    place = fsdp // 2
    low = 1 - place // (p_half // 2)
    passing = []
    for i in range(p_half - 1):
        down = p_half - 1 - i - (place - (p_half - 1 - i) + p_half) // p_half
        up = i + (i - place + p_half) // p_half
        passing.append((low * down + (1 - low) * up - place + p_half) % p_half)

    stat_all[rep] = jnp.zeros(stat_all.shape[1:], F32)
    scores[0] = product(0, n_fsdp, 0, last - 1)
    q_forward(last - 1)
    scores[0] += product(0, n_fsdp, last - 1, last)
    q_forward(last)
    scores[0] += product(0, n_fsdp, last, GROUPS)
    across = p_all.at[0:n_fsdp, 0:pas]
    remote(across, p_all.at[n_fsdp:2 * n_fsdp, 0:pas], p_send, p_core, rep=mate).wait_recv()
    sides = [jnp.where(valid, s * score_scale, -1e30)
             for s in (scores[0], product(n_fsdp, 2 * n_fsdp, 0, GROUPS))]
    scores[0] = sides[0]
    score_send[...] = sides[1]
    top = jnp.maximum(*[jnp.max(s, axis=0, keepdims=True) for s in sides])
    total = sum(jnp.sum(jnp.exp(s - top), axis=0, keepdims=True) for s in sides)
    for k in range(half):
        stat_all[rep, order[k] // 2, 0:1, 0:qry] = top[:, k * qry:(k + 1) * qry]
        stat_all[rep, order[k] // 2, 1:2, 0:qry] = total[:, k * qry:(k + 1) * qry]

    for k in range(1, n_rep):
        remote(stat_all.at[rep], stat_all.at[rep], stat_sem.at[0], stat_sem.at[1],
               rep=(rep + k) % n_rep).start()
    score_copy = remote(score_send, scores.at[1], score_sem.at[0], score_sem.at[1], rep=mate)
    score_copy.start()
    remote(q_all.at[0], q_all.at[half], q_send, q_mate, rep=mate).wait_recv()
    if half > 1:
        ref = q_all.at[half + 1:n_rep]
        remote(ref, ref, q_send, q_far, rep=mate).wait_recv()
    others = pos_all.at[0:n_rep - 1]
    remote(others, others, pos_sem.at[0], pos_sem.at[1], rep=mate).wait()
    others = gain_all.at[0:n_fsdp - 1]
    remote(others, others, gain_sem.at[0], gain_sem.at[1], fsdp=p_mate).wait()
    remote(q_all.at[0:n_rep - 1], q_all.at[0:n_rep - 1], q_send, q_mate, rep=mate).wait_send()
    across = p_all.at[0:2 * n_fsdp - 1, 0:pas]
    remote(across, across, p_send, p_core, rep=mate).wait_send()
    score_copy.wait()
    remote(a_all.at[1:n_fsdp], a_all.at[1:n_fsdp], a_sem.at[0], a_sem.at[1], fsdp=p_mate).wait()
    stats = stat_all.at[0:n_rep - 1]
    remote(stats, stats, stat_sem.at[0], stat_sem.at[1], rep=mate).wait()

    loss_part = jnp.zeros((1, 1), F32)
    weights = []
    for group in range(2):
        blocks = order[group * half:(group + 1) * half]
        from_ = [(mate if group else rep) % 2 + 2 * k for k in range(half)]
        log_totals = []
        for block in blocks:
            tops = [stat_all[r, block // 2, 0:1, 0:qry] for r in from_]
            top = functools.reduce(jnp.maximum, tops)
            total = sum(stat_all[r, block // 2, 1:2, 0:qry] * jnp.exp(t - top)
                        for r, t in zip(from_, tops))
            log_totals.append(top + jnp.log(total))
        s = scores[group]
        match = (pass_ids == jnp.concatenate([pos_all[block] for block in blocks], axis=1)) & valid
        log_total = jnp.concatenate(log_totals, axis=1)
        weights.append(jnp.exp(s - log_total) - jnp.where(match, 1.0, 0.0))
        hit = jnp.sum(jnp.where(match, s, 0.0), axis=0, keepdims=True)
        loss_part = loss_part - jnp.sum(hit, axis=1, keepdims=True)
        if group == 0:
            loss_part = loss_part + jnp.sum(log_totals[0], axis=1, keepdims=True)
    w_all[...] = jnp.concatenate(weights, axis=1).astype(BF16)

    def near_copy(k, cols=slice(None)):
        return remote(near_send.at[k, 0:rest, cols], near_recv.at[k, 0:rest, cols], near_sent,
                      near_got.at[k], fsdp=p_mate)

    cut = dim // 2
    tile = min(1024, cut)
    for c in range(dim // tile):
        cols = slice(c * tile, (c + 1) * tile)
        grad = jnp.dot(w_all[...], q_all[:, :, cols].reshape(n_rep * qry, tile),
                       preferred_element_type=F32) * score_scale
        for k in range(p_half):
            near_send[k, :, cols] = grad[(p_half + k) * PAD:(p_half + k + 1) * PAD].astype(BF16)
        grad_own[:, cols] = grad[0:p_half * PAD]
        for j in range(n_fsdp):
            for r in range(2):
                at = j * PAD + rest + r
                top_own[r, j, :, cols] = grad[at:at + 1]
    for k in passing[0:]:
        near_copy(k).start()

    def folded(own):
        return jnp.concatenate([own[:, :cut], own[:, cut:]], axis=0)

    def flat(pair):
        return jnp.concatenate([pair[0:1], pair[1:2]], axis=1)

    gain_term = jnp.zeros((1, dim), F32)
    for j in range(n_fsdp):
        row = p_all[j, rest:rest + 1, :].astype(F32)
        own = top_own[0, j]
        inner = jnp.sum(row * own, axis=-1, keepdims=True)
        gain_term = gain_term + a_all[j] * (own - row * inner)
    fold = part // 2
    loss_high = loss_part.astype(BF16).astype(F32)
    loss_terms = jnp.broadcast_to(
        jnp.concatenate([loss_high, loss_part - loss_high], axis=0), (2, LANES))
    for f in range(n_fsdp):
        at = f * part
        halves = jnp.concatenate([gain_term[:, at:at + fold], gain_term[:, at + fold:at + part]], axis=0)
        share_send[f] = jnp.concatenate([loss_terms, halves], axis=1).astype(BF16)
    for k in range(half):
        for j in range(n_fsdp):
            if k or j:
                remote(share_send.at[who(j)], share_recv.at[(-k) % half * n_fsdp + mirror(j)],
                       share_sem.at[0], share_sem.at[1],
                       rep=(rep + 2 * k) % n_rep, fsdp=who(j)).start()
    for r in range(2):
        for j in range(1, n_fsdp):
            top_send[r, j] = folded(top_own[r, j]).astype(BF16)
            remote(top_send.at[r, j], top_recv.at[r, mirror(j)], top_sem.at[r], top_sem.at[2 + r],
                   fsdp=who(j)).start()
    near_copy(0).start()

    for k in passing:
        near_copy(k).wait_recv()
        rows = pl.ds(pl.multiple_of(k * PAD, PAD), PAD)
        far_send[k] = (grad_own[rows, :] + near_recv[k].astype(F32)).astype(BF16)
        remote(far_send.at[k, 0:rest], far_recv.at[p_half - k, 0:rest], far_sem.at[0],
               far_sem.at[1], fsdp=(fsdp + 2 * k) % n_fsdp).start()

    def row_sum(r):
        sums = top_recv.at[r, 1:n_fsdp]
        remote(sums, sums, top_sem.at[r], top_sem.at[2 + r], fsdp=p_mate).wait()
        total = folded(top_own[r, 0])
        for j in range(1, n_fsdp):
            total = total + top_recv[r, j].astype(F32)
        return flat(total)

    def final(total, rows):
        row = p_dir[rows, :]
        return (total - row * jnp.sum(row * total, axis=-1, keepdims=True)) * p_inv[rows]

    shares = share_recv.at[1:half * n_fsdp]
    remote(shares, shares, share_sem.at[0], share_sem.at[1], fsdp=p_mate).wait()
    total = share_send[fsdp].astype(F32)
    for f in range(1, half * n_fsdp):
        total = total + share_recv[f].astype(F32)
    total_all[0] = total
    total_copy = remote(total_all.at[0], total_all.at[1], total_sem.at[0], total_sem.at[1], rep=mate)
    total_copy.start()

    top_grad = final(row_sum(0), slice(0, 1))
    pg_out[0:1, :] = top_grad
    slope = top_grad / length
    for f in range(n_fsdp):
        scaled = gain_all[f] * slope[:, f * part:(f + 1) * part]
        wide[:, f * part:(f + 1) * part] = jnp.broadcast_to(scaled, (16, part))

    def inner_pass(i, _):
        rows = pl.ds(pl.multiple_of(i * 16, 16), 16)
        acc = h_in[rows, 0:LANES].astype(F32) * wide[:, 0:LANES]
        for l in range(1, dim // LANES):
            cols = slice(l * LANES, (l + 1) * LANES)
            acc = acc + h_in[rows, cols].astype(F32) * wide[:, cols]
        row_coef[rows, :] = acc
        return 0

    lax.fori_loop(0, length // 16, inner_pass, 0, unroll=4)
    inv = row_inv[...]
    inner = jnp.sum(row_coef[...], axis=-1, keepdims=True)
    row_coef[...] = inner * (inv * inv * inv) / dim

    def last_pass(i, _):
        rows = pl.ds(pl.multiple_of(i * 16, 16), 16)
        inv = row_inv[rows, :]
        coef = row_coef[rows, :]
        for l in range(dim // LANES):
            cols = slice(l * LANES, (l + 1) * LANES)
            h_out[rows, cols] = (wide[:, cols] * inv - h_in[rows, cols].astype(F32) * coef).astype(BF16)
        return 0

    lax.fori_loop(0, length // 16, last_pass, 0, unroll=2)
    pg_out[1:2, :] = final(row_sum(1), slice(1, 2))

    near_copy(0).wait_recv()
    unit_grad = grad_own[0:PAD, :] + near_recv[0].astype(F32)

    total_copy.wait()
    total = total_all[0] + total_all[1]
    gg_out[...] = jnp.concatenate([total[0:1, LANES:], total[1:2, LANES:]], axis=1)
    loss_out[...] = (total[0:1, 0:LANES] + total[1:2, 0:LANES]) / (qry * n_rep * n_fsdp)
    remote(near_send.at[:, 0:rest], near_recv.at[:, 0:rest], near_sent, near_got.at[0],
           fsdp=p_mate).wait_send()

    sums = far_recv.at[1:p_half, 0:rest]
    remote(sums, sums, far_sem.at[0], far_sem.at[1], fsdp=p_mate).wait()
    for k in range(1, p_half):
        unit_grad = unit_grad + far_recv[k].astype(F32)
    pg_out[2:pas, :] = final(unit_grad[0:rest], slice(2, pas))


def write_out(*refs):
    count = (len(refs) - 1) // 2
    sems = refs[-1]
    copies = [pltpu.make_async_copy(refs[i], refs[count + i], sems.at[i]) for i in range(count)]
    for copy in copies:
        copy.start()
    for copy in copies:
        copy.wait()


def per_device(query_cache, passage_cache, positives, norm_gain, hidden_states):
    n_rep, n_fsdp = lax.axis_size("rep"), lax.axis_size("fsdp")
    qry, dim = query_cache.shape
    pas = passage_cache.shape[0]
    length = hidden_states.shape[0]
    part = dim // n_fsdp
    half, p_half = n_rep // 2, n_fsdp // 2
    vmem = pl.BlockSpec(memory_space=pltpu.VMEM)
    hbm = pl.BlockSpec(memory_space=pltpu.HBM)
    dma = pltpu.SemaphoreType.DMA
    results = pl.pallas_call(
        functools.partial(kernel, n_rep, n_fsdp),
        name="step",
        out_shape=(
            pltpu.VMEM((1, LANES), F32),
            pltpu.VMEM((pas, dim), F32),
            pltpu.VMEM((length, dim), BF16),
            pltpu.VMEM((1, part), F32),
        ),
        in_specs=[hbm] * 5,
        out_specs=(vmem, vmem, vmem, vmem),
        scratch_shapes=[
            pltpu.VMEM((qry, dim), BF16),
            pltpu.VMEM((pas, dim), BF16),
            pltpu.VMEM((length, dim), BF16),
            pltpu.VMEM((n_rep, qry, dim), BF16),
            pltpu.VMEM((2 * n_fsdp, PAD, dim), BF16),
            pltpu.VMEM((pas, dim), F32),
            pltpu.VMEM((n_rep, 1, qry), jnp.int32),
            pltpu.VMEM((n_fsdp, 1, part), F32),
            pltpu.VMEM((2, n_fsdp * PAD, half * qry), F32),
            pltpu.VMEM((n_fsdp * PAD, half * qry), F32),
            pltpu.VMEM((n_fsdp * PAD, n_rep * qry), BF16),
            pltpu.VMEM((n_rep, half, 2, LANES), F32),
            pltpu.VMEM((n_fsdp, 1, dim), F32),
            pltpu.VMEM((2, n_fsdp, 1, dim), F32),
            pltpu.VMEM((2, n_fsdp, 2, dim // 2), BF16),
            pltpu.VMEM((2, n_fsdp, 2, dim // 2), BF16),
            pltpu.VMEM((p_half, PAD, dim), BF16),
            pltpu.VMEM((p_half, PAD, dim), BF16),
            pltpu.VMEM((p_half, PAD, dim), BF16),
            pltpu.VMEM((p_half, PAD, dim), BF16),
            pltpu.VMEM((p_half * PAD, dim), F32),
            pltpu.VMEM((n_fsdp, 2, LANES + part // 2), BF16),
            pltpu.VMEM((half * n_fsdp, 2, LANES + part // 2), BF16),
            pltpu.VMEM((2, 2, LANES + part // 2), F32),
            pltpu.VMEM((8, dim), F32),
            pltpu.VMEM((length, LANES), F32),
            pltpu.VMEM((length, LANES), F32),
            pltpu.VMEM((16, dim), F32),
            dma((4,)), dma((qry // 16,)),
            dma, dma((half - 1, GROUPS)), dma, dma,
            dma, dma((p_half - 1,)), dma((p_half,)), dma,
            dma((2,)), dma((2,)), dma((2,)), dma((2,)), dma((2,)), dma((4,)), dma((2,)), dma((2,)),
            dma, dma((p_half,)), dma((2,)),
        ],
        compiler_params=pltpu.CompilerParams(
            collective_id=0, has_side_effects=True, vmem_limit_bytes=40 << 20),
    )(*[pltpu.with_memory_space_constraint(array, pltpu.HBM) for array in (
        query_cache, passage_cache, positives.reshape(1, qry), norm_gain.reshape(1, part),
        hidden_states)])
    loss, passage_grad, hidden_grad, gain_grad = pl.pallas_call(
        write_out,
        name="write_out",
        out_shape=tuple(pltpu.HBM(r.shape, r.dtype) for r in results),
        in_specs=[vmem] * 4,
        out_specs=(hbm,) * 4,
        scratch_shapes=[dma((4,))],
    )(*[pltpu.with_memory_space_constraint(r, pltpu.VMEM) for r in results])
    return loss[0, 0], passage_grad, hidden_grad, gain_grad.reshape(part)


def solution(mesh):
    return jax.shard_map(
        per_device,
        mesh=mesh,
        in_specs=(
            P(("rep", "fsdp"), None),
            P(("rep", "fsdp"), None),
            P(("rep", "fsdp")),
            P("fsdp"),
            P(("rep", "fsdp"), None),
        ),
        out_specs=(P(), P(("rep", "fsdp"), None), P(("rep", "fsdp"), None), P("fsdp")),
        check_vma=False,
    )
```

```python
import functools

import jax
import jax.numpy as jnp
from jax import lax
from jax.experimental import pallas as pl
from jax.experimental.pallas import tpu as pltpu
from jax.sharding import PartitionSpec as P

score_scale = 256.0
PAD = 8
LANES = 128
GROUPS = 4
F32 = jnp.float32
BF16 = jnp.bfloat16


def remote(src, dst, send_sem, recv_sem, **where):
    return pltpu.make_async_remote_copy(
        src_ref=src,
        dst_ref=dst,
        send_sem=send_sem,
        recv_sem=recv_sem,
        device_id=where,
        device_id_type=pl.DeviceIdType.MESH,
    )


def kernel(
    n_rep, n_fsdp, q_hbm, p_hbm, pos_ref, gain_ref, h_hbm,
    loss_out, pg_out, h_out, gg_out,
    q_in, p_in, h_in, q_all, p_all, p_dir, pos_all, gain_all, scores, score_send, w_all, stat_all,
    a_all, top_own, top_send, top_recv, near_send, near_recv, far_send, far_recv, grad_own,
    share_send, share_recv, total_all, col_acc, row_inv, row_coef, wide,
    in_sem, q_sem, q_send, q_near, q_mate, q_far, p_send, p_near, p_far, p_core, pos_sem, gain_sem, a_sem,
    stat_sem, score_sem, top_sem, share_sem, total_sem, near_sent, near_got, far_sem,
):
    rep, fsdp = lax.axis_index("rep"), lax.axis_index("fsdp")
    qry, dim = q_in.shape
    pas = p_in.shape[0]
    length = h_in.shape[0]
    rest = pas - 2
    half = n_rep // 2
    p_half = n_fsdp // 2
    part = dim // n_fsdp
    width = dim // GROUPS
    mate = rep + 1 - 2 * (rep % 2)
    p_mate = fsdp + 1 - 2 * (fsdp % 2)
    odd = (fsdp // 2) % 2

    def turned(k):
        return odd * (p_half - k) + (1 - odd) * k

    barrier = pltpu.get_barrier_semaphore()
    direct = [{"rep": mate}, {"fsdp": p_mate}]
    direct += [{"rep": (rep + 2 * k) % n_rep} for k in range(1, half)]
    direct += [{"fsdp": (fsdp + 2 * k) % n_fsdp} for k in range(1, p_half)]
    for where in direct:
        pl.semaphore_signal(barrier, inc=1, device_id=where, device_id_type=pl.DeviceIdType.MESH)

    q_loads = [
        pltpu.make_async_copy(q_hbm.at[c * 16:(c + 1) * 16], q_in.at[c * 16:(c + 1) * 16], q_sem.at[c])
        for c in range(qry // 16)
    ]
    loads = [
        pltpu.make_async_copy(p_hbm, p_in, in_sem.at[0]),
        pltpu.make_async_copy(pos_ref, pos_all.at[rep], in_sem.at[1]),
        pltpu.make_async_copy(gain_ref, gain_all.at[fsdp], in_sem.at[2]),
        pltpu.make_async_copy(h_hbm, h_in, in_sem.at[3]),
    ]
    for load in q_loads + loads[:3]:
        load.start()

    def who(j):
        return ((fsdp + 2 * j) if j < p_half else (p_mate + 2 * (j - p_half))) % n_fsdp

    def mirror(j):
        return (-j) % p_half if j < p_half else p_half + (-(j - p_half)) % p_half

    for c in range(qry // 16):
        q_loads[c].wait()
        rows = slice(c * 16, (c + 1) * 16)
        raw = q_in[rows, :].astype(F32)
        radius = jnp.sqrt(jnp.sum(raw * raw, axis=-1, keepdims=True) + 1e-06)
        q_all[0, rows, :] = (q_in[rows, :].astype(F32) * (1.0 / radius)).astype(BF16)

    loads[3].start()
    pl.semaphore_wait(barrier, len(direct))

    def cols_of(g):
        return slice(g * width, (g + 1) * width)

    cut = dim // 2

    def p_block(j, h):
        return p_all.at[j, 0:pas, h * cut:(h + 1) * cut]

    for g in range(GROUPS):
        for k in range(1, half):
            remote(q_all.at[0, :, cols_of(g)], q_all.at[half - k, :, cols_of(g)], q_send,
                   q_near.at[half - k - 1, g], rep=(rep + 2 * k) % n_rep).start()
    remote(q_all.at[0], q_all.at[half], q_send, q_mate, rep=mate).start()

    loads[0].wait()
    wide_p = p_in[...].astype(F32)
    p_radius = jnp.sqrt(jnp.sum(wide_p * wide_p, axis=-1, keepdims=True) + 1e-06)
    p_inv = 1.0 / p_radius
    p_dir[...] = wide_p * p_inv
    p_all[0] = jnp.concatenate(
        [p_dir[2:pas], p_dir[0:2], jnp.zeros((PAD - pas, dim), F32)], axis=0).astype(BF16)
    def p_across(j, h):
        remote(p_block(j, h), p_block(n_fsdp + j, h), p_send, p_core.at[h], rep=mate).start()

    for h in range(2):
        for k in range(1, p_half):
            k = turned(k)
            remote(p_block(0, h), p_block(p_half - k, h), p_send, p_near.at[p_half - k - 1, h],
                   fsdp=(fsdp + 2 * k) % n_fsdp).start()
        remote(p_block(0, h), p_block(p_half, h), p_send, p_far.at[0, h], fsdp=p_mate).start()
        p_across(0, h)

    loads[3].wait()
    col_acc[...] = jnp.zeros_like(col_acc)

    def square_pass(i, _):
        rows = pl.ds(pl.multiple_of(i * 16, 16), 16)
        acc = None
        for l in range(dim // LANES):
            x = h_in[rows, l * LANES:(l + 1) * LANES].astype(F32)
            acc = x * x if acc is None else acc + x * x
        row_coef[rows, :] = acc
        return 0

    lax.fori_loop(0, length // 16, square_pass, 0, unroll=4)
    square = jnp.sum(row_coef[...], axis=-1, keepdims=True) / dim
    row_inv[...] = jnp.broadcast_to(1.0 / jnp.sqrt(square + 1e-05), row_inv.shape)

    def column_pass(i, _):
        rows = pl.ds(pl.multiple_of(i * 32, 32), 32)
        inv = row_inv[rows, :]
        for l in range(dim // LANES):
            cols = slice(l * LANES, (l + 1) * LANES)
            y = h_in[rows, cols].astype(F32) * inv
            col_acc[:, cols] += (y[:8] + y[8:16]) + (y[16:24] + y[24:])
        return 0

    lax.fori_loop(0, length // 32, column_pass, 0, unroll=2)
    colsum = jnp.sum(col_acc[...], axis=0, keepdims=True)
    slopes = colsum * (p_inv[0:1] / length)
    a_all[0] = jnp.concatenate([slopes[:, :dim // 2], slopes[:, dim // 2:]], axis=0).astype(BF16)

    def q_forward(g):
        for k in range(1, half):
            ref = q_all.at[k, :, cols_of(g)]
            remote(ref, ref, q_send, q_near.at[k - 1, g], rep=mate).wait_recv()
            remote(ref, q_all.at[half + k, :, cols_of(g)], q_send, q_far,
                   rep=mate).start()

    def p_forward(k, h):
        remote(p_block(k, h), p_block(k, h), p_send, p_near.at[k - 1, h], fsdp=p_mate).wait_recv()
        remote(p_block(k, h), p_block(p_half + k, h), p_send, p_far.at[k, h], fsdp=p_mate).start()
        p_across(k, h)

    def p_last(k, h):
        remote(p_block(k, h), p_block(p_half + k, h), p_send, p_far.at[k, h], fsdp=p_mate).wait_recv()
        p_across(p_half + k, h)

    for h in range(2):
        for k in range(1, p_half):
            p_forward(turned(k), h)
    loads[1].wait()
    loads[2].wait()
    for k in range(1, n_fsdp):
        remote(gain_all.at[fsdp], gain_all.at[fsdp], gain_sem.at[0], gain_sem.at[1],
               fsdp=(fsdp + k) % n_fsdp).start()
    last = GROUPS - 1
    p_last(0, 0)
    p_last(0, 1)
    for g in range(last - 1):
        q_forward(g)
    for k in range(1, n_rep):
        remote(pos_all.at[rep], pos_all.at[rep], pos_sem.at[0], pos_sem.at[1],
               rep=(rep + k) % n_rep).start()
    for h in range(2):
        for k in range(1, p_half):
            p_last(turned(k), h)
    for j in range(1, n_fsdp):
        remote(a_all.at[0], a_all.at[mirror(j)], a_sem.at[0], a_sem.at[1], fsdp=who(j)).start()

    rows_all = n_fsdp * PAD
    own_qry = half * qry
    slot = lax.broadcasted_iota(jnp.int32, (rows_all, own_qry), 0)
    lane = slot % PAD
    valid = lane < pas
    index = slot // PAD
    source = jnp.where(index < p_half, fsdp + 2 * index, p_mate + 2 * (index - p_half))
    source = jnp.where(source >= n_fsdp, source - n_fsdp, source)
    pass_ids = (rep * n_fsdp + source) * pas + jnp.where(lane < rest, lane + 2, lane - rest)

    order = [(rep + 2 * k) % n_rep for k in range(half)] + [(mate + 2 * k) % n_rep for k in range(half)]

    def product(first, end, g0, g1):
        cols = slice(g0 * width, g1 * width)
        rows = p_all[first:end, :, cols].reshape((end - first) * PAD, (g1 - g0) * width)
        return lax.dot_general(rows, q_all[0:half, :, cols].reshape(own_qry, (g1 - g0) * width),
                               (((1,), (1,)), ((), ())), preferred_element_type=F32)

    place = fsdp // 2
    low = 1 - place // (p_half // 2)
    passing = []
    for i in range(p_half - 1):
        down = p_half - 1 - i - (place - (p_half - 1 - i) + p_half) // p_half
        up = i + (i - place + p_half) // p_half
        passing.append((low * down + (1 - low) * up - place + p_half) % p_half)

    stat_all[rep] = jnp.zeros(stat_all.shape[1:], F32)
    scores[0] = product(0, n_fsdp, 0, last - 1)
    q_forward(last - 1)
    scores[0] += product(0, n_fsdp, last - 1, last)
    def p_core_wait(h):
        cols = slice(h * cut, (h + 1) * cut)
        remote(p_all.at[0:n_fsdp, 0:pas, cols], p_all.at[n_fsdp:2 * n_fsdp, 0:pas, cols], p_send,
               p_core.at[h], rep=mate).wait_recv()

    p_core_wait(0)
    score_send[...] = product(n_fsdp, 2 * n_fsdp, 0, GROUPS // 2)
    q_forward(last)
    scores[0] += product(0, n_fsdp, last, GROUPS)
    p_core_wait(1)
    mate_part = score_send[...] + product(n_fsdp, 2 * n_fsdp, GROUPS // 2, GROUPS)
    sides = [jnp.where(valid, s * score_scale, -1e30) for s in (scores[0], mate_part)]
    scores[0] = sides[0]
    score_send[...] = sides[1]
    top = jnp.maximum(*[jnp.max(s, axis=0, keepdims=True) for s in sides])
    total = sum(jnp.sum(jnp.exp(s - top), axis=0, keepdims=True) for s in sides)
    for k in range(half):
        stat_all[rep, order[k] // 2, 0:1, 0:qry] = top[:, k * qry:(k + 1) * qry]
        stat_all[rep, order[k] // 2, 1:2, 0:qry] = total[:, k * qry:(k + 1) * qry]

    for k in range(1, n_rep):
        remote(stat_all.at[rep], stat_all.at[rep], stat_sem.at[0], stat_sem.at[1],
               rep=(rep + k) % n_rep).start()
    score_copy = remote(score_send, scores.at[1], score_sem.at[0], score_sem.at[1], rep=mate)
    score_copy.start()
    remote(q_all.at[0], q_all.at[half], q_send, q_mate, rep=mate).wait_recv()
    if half > 1:
        ref = q_all.at[half + 1:n_rep]
        remote(ref, ref, q_send, q_far, rep=mate).wait_recv()
    others = pos_all.at[0:n_rep - 1]
    remote(others, others, pos_sem.at[0], pos_sem.at[1], rep=mate).wait()
    others = gain_all.at[0:n_fsdp - 1]
    remote(others, others, gain_sem.at[0], gain_sem.at[1], fsdp=p_mate).wait()
    remote(q_all.at[0:n_rep - 1], q_all.at[0:n_rep - 1], q_send, q_mate, rep=mate).wait_send()
    across = p_all.at[0:2 * n_fsdp - 1, 0:pas]
    remote(across, across, p_send, p_core.at[0], rep=mate).wait_send()
    score_copy.wait()
    stats = stat_all.at[0:n_rep - 1]
    remote(stats, stats, stat_sem.at[0], stat_sem.at[1], rep=mate).wait()

    loss_part = jnp.zeros((1, 1), F32)
    weights = []
    for group in range(2):
        blocks = order[group * half:(group + 1) * half]
        from_ = [(mate if group else rep) % 2 + 2 * k for k in range(half)]
        log_totals = []
        for block in blocks:
            tops = [stat_all[r, block // 2, 0:1, 0:qry] for r in from_]
            top = functools.reduce(jnp.maximum, tops)
            total = sum(stat_all[r, block // 2, 1:2, 0:qry] * jnp.exp(t - top)
                        for r, t in zip(from_, tops))
            log_totals.append(top + jnp.log(total))
        s = scores[group]
        match = (pass_ids == jnp.concatenate([pos_all[block] for block in blocks], axis=1)) & valid
        log_total = jnp.concatenate(log_totals, axis=1)
        weights.append(jnp.exp(s - log_total) - jnp.where(match, 1.0, 0.0))
        hit = jnp.sum(jnp.where(match, s, 0.0), axis=0, keepdims=True)
        loss_part = loss_part - jnp.sum(hit, axis=1, keepdims=True)
        if group == 0:
            loss_part = loss_part + jnp.sum(log_totals[0], axis=1, keepdims=True)
    w_all[...] = jnp.concatenate(weights, axis=1).astype(BF16)

    def near_copy(k, cols=slice(None)):
        return remote(near_send.at[k, 0:rest, cols], near_recv.at[k, 0:rest, cols], near_sent,
                      near_got.at[k], fsdp=p_mate)

    tile = min(1024, cut)
    for c in range(dim // tile):
        cols = slice(c * tile, (c + 1) * tile)
        grad = jnp.dot(w_all[...], q_all[:, :, cols].reshape(n_rep * qry, tile),
                       preferred_element_type=F32) * score_scale
        for k in range(p_half):
            near_send[k, :, cols] = grad[(p_half + k) * PAD:(p_half + k + 1) * PAD].astype(BF16)
        grad_own[:, cols] = grad[0:p_half * PAD]
        for j in range(n_fsdp):
            for r in range(2):
                at = j * PAD + rest + r
                top_own[r, j, :, cols] = grad[at:at + 1]
    for k in passing[0:]:
        near_copy(k).start()

    def folded(own):
        return jnp.concatenate([own[:, :cut], own[:, cut:]], axis=0)

    def flat(pair):
        return jnp.concatenate([pair[0:1], pair[1:2]], axis=1)

    remote(a_all.at[1:n_fsdp], a_all.at[1:n_fsdp], a_sem.at[0], a_sem.at[1], fsdp=p_mate).wait()
    gain_term = jnp.zeros((2, cut), F32)
    for j in range(n_fsdp):
        row = p_all[j, rest:rest + 1, :].astype(F32)
        own = top_own[0, j]
        inner = jnp.sum(row * own, axis=-1, keepdims=True)
        gain_term = gain_term + a_all[j].astype(F32) * folded(own - row * inner)
    fold = part // 2
    loss_high = loss_part.astype(BF16).astype(F32)
    loss_terms = jnp.broadcast_to(
        jnp.concatenate([loss_high, loss_part - loss_high], axis=0), (2, LANES))
    gain_term = flat(gain_term)
    for f in range(n_fsdp):
        at = f * part
        halves = jnp.concatenate([gain_term[:, at:at + fold], gain_term[:, at + fold:at + part]], axis=0)
        share_send[f] = jnp.concatenate([loss_terms, halves], axis=1).astype(BF16)
    for k in range(half):
        for j in range(n_fsdp):
            if k or j:
                remote(share_send.at[who(j)], share_recv.at[(-k) % half * n_fsdp + mirror(j)],
                       share_sem.at[0], share_sem.at[1],
                       rep=(rep + 2 * k) % n_rep, fsdp=who(j)).start()
    for r in range(2):
        for j in range(1, n_fsdp):
            top_send[r, j] = folded(top_own[r, j]).astype(BF16)
            remote(top_send.at[r, j], top_recv.at[r, mirror(j)], top_sem.at[r], top_sem.at[2 + r],
                   fsdp=who(j)).start()
    near_copy(0).start()

    for k in passing:
        near_copy(k).wait_recv()
        rows = pl.ds(pl.multiple_of(k * PAD, PAD), PAD)
        far_send[k] = (grad_own[rows, :] + near_recv[k].astype(F32)).astype(BF16)
        remote(far_send.at[k, 0:rest], far_recv.at[p_half - k, 0:rest], far_sem.at[0],
               far_sem.at[1], fsdp=(fsdp + 2 * k) % n_fsdp).start()

    def row_sum(r):
        sums = top_recv.at[r, 1:n_fsdp]
        remote(sums, sums, top_sem.at[r], top_sem.at[2 + r], fsdp=p_mate).wait()
        total = folded(top_own[r, 0])
        for j in range(1, n_fsdp):
            total = total + top_recv[r, j].astype(F32)
        return flat(total)

    def final(total, rows):
        row = p_dir[rows, :]
        return (total - row * jnp.sum(row * total, axis=-1, keepdims=True)) * p_inv[rows]

    shares = share_recv.at[1:half * n_fsdp]
    remote(shares, shares, share_sem.at[0], share_sem.at[1], fsdp=p_mate).wait()
    total = share_send[fsdp].astype(F32)
    for f in range(1, half * n_fsdp):
        total = total + share_recv[f].astype(F32)
    total_all[0] = total
    total_copy = remote(total_all.at[0], total_all.at[1], total_sem.at[0], total_sem.at[1], rep=mate)
    total_copy.start()

    top_grad = final(row_sum(0), slice(0, 1))
    pg_out[0:1, :] = top_grad
    slope = top_grad / length
    for f in range(n_fsdp):
        scaled = gain_all[f] * slope[:, f * part:(f + 1) * part]
        wide[:, f * part:(f + 1) * part] = jnp.broadcast_to(scaled, (16, part))

    def inner_pass(i, _):
        rows = pl.ds(pl.multiple_of(i * 16, 16), 16)
        acc = h_in[rows, 0:LANES].astype(F32) * wide[:, 0:LANES]
        for l in range(1, dim // LANES):
            cols = slice(l * LANES, (l + 1) * LANES)
            acc = acc + h_in[rows, cols].astype(F32) * wide[:, cols]
        row_coef[rows, :] = acc
        return 0

    lax.fori_loop(0, length // 16, inner_pass, 0, unroll=4)
    inv = row_inv[...]
    inner = jnp.sum(row_coef[...], axis=-1, keepdims=True)
    row_coef[...] = inner * (inv * inv * inv) / dim

    def last_pass(i, _):
        rows = pl.ds(pl.multiple_of(i * 16, 16), 16)
        inv = row_inv[rows, :]
        coef = row_coef[rows, :]
        for l in range(dim // LANES):
            cols = slice(l * LANES, (l + 1) * LANES)
            h_out[rows, cols] = (wide[:, cols] * inv - h_in[rows, cols].astype(F32) * coef).astype(BF16)
        return 0

    lax.fori_loop(0, length // 16, last_pass, 0, unroll=2)
    pg_out[1:2, :] = final(row_sum(1), slice(1, 2))

    near_copy(0).wait_recv()
    unit_grad = grad_own[0:PAD, :] + near_recv[0].astype(F32)

    total_copy.wait()
    total = total_all[0] + total_all[1]
    gg_out[...] = jnp.concatenate([total[0:1, LANES:], total[1:2, LANES:]], axis=1)
    loss_out[...] = (total[0:1, 0:LANES] + total[1:2, 0:LANES]) / (qry * n_rep * n_fsdp)
    remote(near_send.at[:, 0:rest], near_recv.at[:, 0:rest], near_sent, near_got.at[0],
           fsdp=p_mate).wait_send()

    sums = far_recv.at[1:p_half, 0:rest]
    remote(sums, sums, far_sem.at[0], far_sem.at[1], fsdp=p_mate).wait()
    for k in range(1, p_half):
        unit_grad = unit_grad + far_recv[k].astype(F32)
    pg_out[2:pas, :] = final(unit_grad[0:rest], slice(2, pas))


def write_out(*refs):
    count = (len(refs) - 1) // 2
    sems = refs[-1]
    copies = [pltpu.make_async_copy(refs[i], refs[count + i], sems.at[i]) for i in range(count)]
    for copy in copies:
        copy.start()
    for copy in copies:
        copy.wait()


def per_device(query_cache, passage_cache, positives, norm_gain, hidden_states):
    n_rep, n_fsdp = lax.axis_size("rep"), lax.axis_size("fsdp")
    qry, dim = query_cache.shape
    pas = passage_cache.shape[0]
    length = hidden_states.shape[0]
    part = dim // n_fsdp
    half, p_half = n_rep // 2, n_fsdp // 2
    vmem = pl.BlockSpec(memory_space=pltpu.VMEM)
    hbm = pl.BlockSpec(memory_space=pltpu.HBM)
    dma = pltpu.SemaphoreType.DMA
    results = pl.pallas_call(
        functools.partial(kernel, n_rep, n_fsdp),
        name="step",
        out_shape=(
            pltpu.VMEM((1, LANES), F32),
            pltpu.VMEM((pas, dim), F32),
            pltpu.VMEM((length, dim), BF16),
            pltpu.VMEM((1, part), F32),
        ),
        in_specs=[hbm] * 5,
        out_specs=(vmem, vmem, vmem, vmem),
        scratch_shapes=[
            pltpu.VMEM((qry, dim), BF16),
            pltpu.VMEM((pas, dim), BF16),
            pltpu.VMEM((length, dim), BF16),
            pltpu.VMEM((n_rep, qry, dim), BF16),
            pltpu.VMEM((2 * n_fsdp, PAD, dim), BF16),
            pltpu.VMEM((pas, dim), F32),
            pltpu.VMEM((n_rep, 1, qry), jnp.int32),
            pltpu.VMEM((n_fsdp, 1, part), F32),
            pltpu.VMEM((2, n_fsdp * PAD, half * qry), F32),
            pltpu.VMEM((n_fsdp * PAD, half * qry), F32),
            pltpu.VMEM((n_fsdp * PAD, n_rep * qry), BF16),
            pltpu.VMEM((n_rep, half, 2, LANES), F32),
            pltpu.VMEM((n_fsdp, 2, dim // 2), BF16),
            pltpu.VMEM((2, n_fsdp, 1, dim), F32),
            pltpu.VMEM((2, n_fsdp, 2, dim // 2), BF16),
            pltpu.VMEM((2, n_fsdp, 2, dim // 2), BF16),
            pltpu.VMEM((p_half, PAD, dim), BF16),
            pltpu.VMEM((p_half, PAD, dim), BF16),
            pltpu.VMEM((p_half, PAD, dim), BF16),
            pltpu.VMEM((p_half, PAD, dim), BF16),
            pltpu.VMEM((p_half * PAD, dim), F32),
            pltpu.VMEM((n_fsdp, 2, LANES + part // 2), BF16),
            pltpu.VMEM((half * n_fsdp, 2, LANES + part // 2), BF16),
            pltpu.VMEM((2, 2, LANES + part // 2), F32),
            pltpu.VMEM((8, dim), F32),
            pltpu.VMEM((length, LANES), F32),
            pltpu.VMEM((length, LANES), F32),
            pltpu.VMEM((16, dim), F32),
            dma((4,)), dma((qry // 16,)),
            dma, dma((half - 1, GROUPS)), dma, dma,
            dma, dma((p_half - 1, 2)), dma((p_half, 2)), dma((2,)),
            dma((2,)), dma((2,)), dma((2,)), dma((2,)), dma((2,)), dma((4,)), dma((2,)), dma((2,)),
            dma, dma((p_half,)), dma((2,)),
        ],
        compiler_params=pltpu.CompilerParams(
            collective_id=0, has_side_effects=True, vmem_limit_bytes=40 << 20),
    )(*[pltpu.with_memory_space_constraint(array, pltpu.HBM) for array in (
        query_cache, passage_cache, positives.reshape(1, qry), norm_gain.reshape(1, part),
        hidden_states)])
    loss, passage_grad, hidden_grad, gain_grad = pl.pallas_call(
        write_out,
        name="write_out",
        out_shape=tuple(pltpu.HBM(r.shape, r.dtype) for r in results),
        in_specs=[vmem] * 4,
        out_specs=(hbm,) * 4,
        scratch_shapes=[dma((4,))],
    )(*[pltpu.with_memory_space_constraint(r, pltpu.VMEM) for r in results])
    return loss[0, 0], passage_grad, hidden_grad, gain_grad.reshape(part)


def solution(mesh):
    return jax.shard_map(
        per_device,
        mesh=mesh,
        in_specs=(
            P(("rep", "fsdp"), None),
            P(("rep", "fsdp"), None),
            P(("rep", "fsdp")),
            P("fsdp"),
            P(("rep", "fsdp"), None),
        ),
        out_specs=(P(), P(("rep", "fsdp"), None), P(("rep", "fsdp"), None), P("fsdp")),
        check_vma=False,
    )
```

```python
import functools

import jax
import jax.numpy as jnp
from jax import lax
from jax.experimental import pallas as pl
from jax.experimental.pallas import tpu as pltpu
from jax.sharding import PartitionSpec as P

score_scale = 256.0
PAD = 8
LANES = 128
GROUPS = 4
F32 = jnp.float32
BF16 = jnp.bfloat16


def remote(src, dst, send_sem, recv_sem, **where):
    return pltpu.make_async_remote_copy(
        src_ref=src,
        dst_ref=dst,
        send_sem=send_sem,
        recv_sem=recv_sem,
        device_id=where,
        device_id_type=pl.DeviceIdType.MESH,
    )


def kernel(
    n_rep, n_fsdp, q_hbm, p_hbm, pos_ref, gain_ref, h_hbm,
    loss_out, pg_out, h_out, gg_out,
    q_in, p_in, h_in, q_all, p_all, p_dir, pos_all, gain_all, scores, score_send, w_all, stat_all,
    a_all, top_own, top_send, top_recv, near_send, near_recv, far_send, far_recv, grad_own,
    share_send, share_recv, total_all, col_acc, row_inv, row_coef, wide,
    in_sem, q_sem, q_send, q_near, q_mate, q_far, p_send, p_near, p_far, p_core, pos_sem, gain_sem, a_sem,
    stat_sem, score_sem, top_sem, share_sem, total_sem, near_sent, near_got, far_sem,
):
    rep, fsdp = lax.axis_index("rep"), lax.axis_index("fsdp")
    qry, dim = q_in.shape
    pas = p_in.shape[0]
    length = h_in.shape[0]
    rest = pas - 2
    half = n_rep // 2
    p_half = n_fsdp // 2
    part = dim // n_fsdp
    width = dim // GROUPS
    mate = rep + 1 - 2 * (rep % 2)
    p_mate = fsdp + 1 - 2 * (fsdp % 2)
    odd = (fsdp // 2) % 2

    def turned(k):
        return odd * (p_half - k) + (1 - odd) * k

    barrier = pltpu.get_barrier_semaphore()
    direct = [{"rep": mate}, {"fsdp": p_mate}]
    direct += [{"rep": (rep + 2 * k) % n_rep} for k in range(1, half)]
    direct += [{"fsdp": (fsdp + 2 * k) % n_fsdp} for k in range(1, p_half)]
    for where in direct:
        pl.semaphore_signal(barrier, inc=1, device_id=where, device_id_type=pl.DeviceIdType.MESH)

    q_loads = [
        pltpu.make_async_copy(q_hbm.at[c * 16:(c + 1) * 16], q_in.at[c * 16:(c + 1) * 16], q_sem.at[c])
        for c in range(qry // 16)
    ]
    loads = [
        pltpu.make_async_copy(p_hbm, p_in, in_sem.at[0]),
        pltpu.make_async_copy(pos_ref, pos_all.at[rep], in_sem.at[1]),
        pltpu.make_async_copy(gain_ref, gain_all.at[fsdp], in_sem.at[2]),
        pltpu.make_async_copy(h_hbm, h_in, in_sem.at[3]),
    ]
    for load in q_loads + loads[:3]:
        load.start()

    def who(j):
        return ((fsdp + 2 * j) if j < p_half else (p_mate + 2 * (j - p_half))) % n_fsdp

    def mirror(j):
        return (-j) % p_half if j < p_half else p_half + (-(j - p_half)) % p_half

    for c in range(qry // 16):
        q_loads[c].wait()
        rows = slice(c * 16, (c + 1) * 16)
        raw = q_in[rows, :].astype(F32)
        radius = jnp.sqrt(jnp.sum(raw * raw, axis=-1, keepdims=True) + 1e-06)
        q_all[0, rows, :] = (q_in[rows, :].astype(F32) * (1.0 / radius)).astype(BF16)

    loads[3].start()
    pl.semaphore_wait(barrier, len(direct))

    def cols_of(g):
        return slice(g * width, (g + 1) * width)

    cut = dim // 2

    def p_block(j, h):
        return p_all.at[j, 0:pas, h * cut:(h + 1) * cut]

    for g in range(GROUPS):
        for k in range(1, half):
            remote(q_all.at[0, :, cols_of(g)], q_all.at[half - k, :, cols_of(g)], q_send,
                   q_near.at[half - k - 1, g], rep=(rep + 2 * k) % n_rep).start()
    remote(q_all.at[0], q_all.at[half], q_send, q_mate, rep=mate).start()

    loads[0].wait()
    wide_p = p_in[...].astype(F32)
    p_radius = jnp.sqrt(jnp.sum(wide_p * wide_p, axis=-1, keepdims=True) + 1e-06)
    p_inv = 1.0 / p_radius
    p_dir[...] = wide_p * p_inv
    p_all[0] = jnp.concatenate(
        [p_dir[2:pas], p_dir[0:2], jnp.zeros((PAD - pas, dim), F32)], axis=0).astype(BF16)
    def p_across(j, h):
        remote(p_block(j, h), p_block(n_fsdp + j, h), p_send, p_core.at[h], rep=mate).start()

    for h in range(2):
        for k in range(1, p_half):
            k = turned(k)
            remote(p_block(0, h), p_block(p_half - k, h), p_send, p_near.at[p_half - k - 1, h],
                   fsdp=(fsdp + 2 * k) % n_fsdp).start()
        remote(p_block(0, h), p_block(p_half, h), p_send, p_far.at[0, h], fsdp=p_mate).start()
        p_across(0, h)

    loads[3].wait()
    col_acc[...] = jnp.zeros_like(col_acc)

    def square_pass(i, _):
        rows = pl.ds(pl.multiple_of(i * 16, 16), 16)
        acc = None
        for l in range(dim // LANES):
            x = h_in[rows, l * LANES:(l + 1) * LANES].astype(F32)
            acc = x * x if acc is None else acc + x * x
        row_coef[rows, :] = acc
        return 0

    lax.fori_loop(0, length // 16, square_pass, 0, unroll=4)
    square = jnp.sum(row_coef[...], axis=-1, keepdims=True) / dim
    row_inv[...] = jnp.broadcast_to(1.0 / jnp.sqrt(square + 1e-05), row_inv.shape)

    def column_pass(i, _):
        rows = pl.ds(pl.multiple_of(i * 32, 32), 32)
        inv = row_inv[rows, :]
        for l in range(dim // LANES):
            cols = slice(l * LANES, (l + 1) * LANES)
            y = h_in[rows, cols].astype(F32) * inv
            col_acc[:, cols] += (y[:8] + y[8:16]) + (y[16:24] + y[24:])
        return 0

    lax.fori_loop(0, length // 32, column_pass, 0, unroll=2)
    colsum = jnp.sum(col_acc[...], axis=0, keepdims=True)
    slopes = colsum * (p_inv[0:1] / length)
    a_all[0] = jnp.concatenate([slopes[:, :dim // 2], slopes[:, dim // 2:]], axis=0).astype(BF16)

    def q_forward(g):
        for k in range(1, half):
            ref = q_all.at[k, :, cols_of(g)]
            remote(ref, ref, q_send, q_near.at[k - 1, g], rep=mate).wait_recv()
            remote(ref, q_all.at[half + k, :, cols_of(g)], q_send, q_far,
                   rep=mate).start()

    def p_forward(k, h):
        remote(p_block(k, h), p_block(k, h), p_send, p_near.at[k - 1, h], fsdp=p_mate).wait_recv()
        remote(p_block(k, h), p_block(p_half + k, h), p_send, p_far.at[k, h], fsdp=p_mate).start()
        p_across(k, h)

    def p_last(k, h):
        remote(p_block(k, h), p_block(p_half + k, h), p_send, p_far.at[k, h], fsdp=p_mate).wait_recv()
        p_across(p_half + k, h)

    for h in range(2):
        for k in range(1, p_half):
            p_forward(turned(k), h)
    loads[1].wait()
    loads[2].wait()
    for k in range(1, n_fsdp):
        remote(gain_all.at[fsdp], gain_all.at[fsdp], gain_sem.at[0], gain_sem.at[1],
               fsdp=(fsdp + k) % n_fsdp).start()
    last = GROUPS - 1
    p_last(0, 0)
    p_last(0, 1)
    for g in range(last - 1):
        q_forward(g)
    for k in range(1, n_rep):
        remote(pos_all.at[rep], pos_all.at[rep], pos_sem.at[0], pos_sem.at[1],
               rep=(rep + k) % n_rep).start()
    for h in range(2):
        for k in range(1, p_half):
            p_last(turned(k), h)
    for j in range(1, n_fsdp):
        remote(a_all.at[0], a_all.at[mirror(j)], a_sem.at[0], a_sem.at[1], fsdp=who(j)).start()

    rows_all = n_fsdp * PAD
    own_qry = half * qry
    slot = lax.broadcasted_iota(jnp.int32, (rows_all, own_qry), 0)
    lane = slot % PAD
    valid = lane < pas
    index = slot // PAD
    source = jnp.where(index < p_half, fsdp + 2 * index, p_mate + 2 * (index - p_half))
    source = jnp.where(source >= n_fsdp, source - n_fsdp, source)
    pass_ids = (rep * n_fsdp + source) * pas + jnp.where(lane < rest, lane + 2, lane - rest)

    order = [(rep + 2 * k) % n_rep for k in range(half)] + [(mate + 2 * k) % n_rep for k in range(half)]

    def product(first, end, g0, g1):
        cols = slice(g0 * width, g1 * width)
        rows = p_all[first:end, :, cols].reshape((end - first) * PAD, (g1 - g0) * width)
        return lax.dot_general(rows, q_all[0:half, :, cols].reshape(own_qry, (g1 - g0) * width),
                               (((1,), (1,)), ((), ())), preferred_element_type=F32)

    place = fsdp // 2
    low = 1 - place // (p_half // 2)
    passing = []
    for i in range(p_half - 1):
        down = p_half - 1 - i - (place - (p_half - 1 - i) + p_half) // p_half
        up = i + (i - place + p_half) // p_half
        passing.append((low * down + (1 - low) * up - place + p_half) % p_half)

    stat_all[rep] = jnp.zeros(stat_all.shape[1:], F32)
    scores[0] = product(0, n_fsdp, 0, last - 1)
    q_forward(last - 1)
    scores[0] += product(0, n_fsdp, last - 1, last)
    def p_core_wait(h):
        cols = slice(h * cut, (h + 1) * cut)
        remote(p_all.at[0:n_fsdp, 0:pas, cols], p_all.at[n_fsdp:2 * n_fsdp, 0:pas, cols], p_send,
               p_core.at[h], rep=mate).wait_recv()

    p_core_wait(0)
    score_send[...] = product(n_fsdp, 2 * n_fsdp, 0, GROUPS // 2)
    q_forward(last)
    scores[0] += product(0, n_fsdp, last, GROUPS)
    p_core_wait(1)
    mate_part = score_send[...] + product(n_fsdp, 2 * n_fsdp, GROUPS // 2, GROUPS)
    sides = [jnp.where(valid, s * score_scale, -1e30) for s in (scores[0], mate_part)]
    scores[0] = sides[0]
    score_send[...] = sides[1]
    top = jnp.maximum(*[jnp.max(s, axis=0, keepdims=True) for s in sides])
    total = sum(jnp.sum(jnp.exp(s - top), axis=0, keepdims=True) for s in sides)
    for k in range(half):
        stat_all[rep, order[k] // 2, 0:1, 0:qry] = top[:, k * qry:(k + 1) * qry]
        stat_all[rep, order[k] // 2, 1:2, 0:qry] = total[:, k * qry:(k + 1) * qry]

    for k in range(1, n_rep):
        remote(stat_all.at[rep], stat_all.at[rep], stat_sem.at[0], stat_sem.at[1],
               rep=(rep + k) % n_rep).start()
    score_copy = remote(score_send, scores.at[1], score_sem.at[0], score_sem.at[1], rep=mate)
    score_copy.start()
    remote(q_all.at[0], q_all.at[half], q_send, q_mate, rep=mate).wait_recv()
    if half > 1:
        ref = q_all.at[half + 1:n_rep]
        remote(ref, ref, q_send, q_far, rep=mate).wait_recv()
    others = pos_all.at[0:n_rep - 1]
    remote(others, others, pos_sem.at[0], pos_sem.at[1], rep=mate).wait()
    others = gain_all.at[0:n_fsdp - 1]
    remote(others, others, gain_sem.at[0], gain_sem.at[1], fsdp=p_mate).wait()
    remote(q_all.at[0:n_rep - 1], q_all.at[0:n_rep - 1], q_send, q_mate, rep=mate).wait_send()
    across = p_all.at[0:2 * n_fsdp - 1, 0:pas]
    remote(across, across, p_send, p_core.at[0], rep=mate).wait_send()
    score_copy.wait()
    stats = stat_all.at[0:n_rep - 1]
    remote(stats, stats, stat_sem.at[0], stat_sem.at[1], rep=mate).wait()

    loss_part = jnp.zeros((1, 1), F32)
    weights = []
    for group in range(2):
        blocks = order[group * half:(group + 1) * half]
        from_ = [(mate if group else rep) % 2 + 2 * k for k in range(half)]
        log_totals = []
        for block in blocks:
            tops = [stat_all[r, block // 2, 0:1, 0:qry] for r in from_]
            top = functools.reduce(jnp.maximum, tops)
            total = sum(stat_all[r, block // 2, 1:2, 0:qry] * jnp.exp(t - top)
                        for r, t in zip(from_, tops))
            log_totals.append(top + jnp.log(total))
        s = scores[group]
        match = (pass_ids == jnp.concatenate([pos_all[block] for block in blocks], axis=1)) & valid
        log_total = jnp.concatenate(log_totals, axis=1)
        weights.append(jnp.exp(s - log_total) - jnp.where(match, 1.0, 0.0))
        hit = jnp.sum(jnp.where(match, s, 0.0), axis=0, keepdims=True)
        loss_part = loss_part - jnp.sum(hit, axis=1, keepdims=True)
        if group == 0:
            loss_part = loss_part + jnp.sum(log_totals[0], axis=1, keepdims=True)
    w_all[...] = jnp.concatenate(weights, axis=1).astype(BF16)

    def near_copy(k, cols=slice(None)):
        return remote(near_send.at[k, 0:rest, cols], near_recv.at[k, 0:rest, cols], near_sent,
                      near_got.at[k], fsdp=p_mate)

    tile = min(1024, cut)
    for c in range(dim // tile):
        cols = slice(c * tile, (c + 1) * tile)
        grad = jnp.dot(w_all[...], q_all[:, :, cols].reshape(n_rep * qry, tile),
                       preferred_element_type=F32) * score_scale
        for k in range(p_half):
            near_send[k, :, cols] = grad[(p_half + k) * PAD:(p_half + k + 1) * PAD].astype(BF16)
        grad_own[:, cols] = grad[0:p_half * PAD]
        for j in range(n_fsdp):
            for r in range(2):
                at = j * PAD + rest + r
                top_own[r, j, :, cols] = grad[at:at + 1]
    for k in passing[0:]:
        near_copy(k).start()

    def folded(own):
        return jnp.concatenate([own[:, :cut], own[:, cut:]], axis=0)

    def flat(pair):
        return jnp.concatenate([pair[0:1], pair[1:2]], axis=1)

    def send_rows(r):
        for j in range(1, n_fsdp):
            top_send[r, j] = folded(top_own[r, j]).astype(BF16)
            remote(top_send.at[r, j], top_recv.at[r, mirror(j)], top_sem.at[r], top_sem.at[2 + r],
                   fsdp=who(j)).start()

    send_rows(0)
    remote(a_all.at[1:n_fsdp], a_all.at[1:n_fsdp], a_sem.at[0], a_sem.at[1], fsdp=p_mate).wait()
    gain_term = jnp.zeros((2, cut), F32)
    for j in range(n_fsdp):
        row = p_all[j, rest:rest + 1, :].astype(F32)
        own = top_own[0, j]
        inner = jnp.sum(row * own, axis=-1, keepdims=True)
        gain_term = gain_term + a_all[j].astype(F32) * folded(own - row * inner)
    fold = part // 2
    loss_high = loss_part.astype(BF16).astype(F32)
    loss_terms = jnp.broadcast_to(
        jnp.concatenate([loss_high, loss_part - loss_high], axis=0), (2, LANES))
    gain_term = flat(gain_term)
    for f in range(n_fsdp):
        at = f * part
        halves = jnp.concatenate([gain_term[:, at:at + fold], gain_term[:, at + fold:at + part]], axis=0)
        share_send[f] = jnp.concatenate([loss_terms, halves], axis=1).astype(BF16)
    for k in range(half):
        for j in range(n_fsdp):
            if k or j:
                remote(share_send.at[who(j)], share_recv.at[(-k) % half * n_fsdp + mirror(j)],
                       share_sem.at[0], share_sem.at[1],
                       rep=(rep + 2 * k) % n_rep, fsdp=who(j)).start()
    send_rows(1)
    near_copy(0).start()

    for k in passing:
        near_copy(k).wait_recv()
        rows = pl.ds(pl.multiple_of(k * PAD, PAD), PAD)
        far_send[k] = (grad_own[rows, :] + near_recv[k].astype(F32)).astype(BF16)
        remote(far_send.at[k, 0:rest], far_recv.at[p_half - k, 0:rest], far_sem.at[0],
               far_sem.at[1], fsdp=(fsdp + 2 * k) % n_fsdp).start()

    def row_sum(r):
        sums = top_recv.at[r, 1:n_fsdp]
        remote(sums, sums, top_sem.at[r], top_sem.at[2 + r], fsdp=p_mate).wait()
        total = folded(top_own[r, 0])
        for j in range(1, n_fsdp):
            total = total + top_recv[r, j].astype(F32)
        return flat(total)

    def final(total, rows):
        row = p_dir[rows, :]
        return (total - row * jnp.sum(row * total, axis=-1, keepdims=True)) * p_inv[rows]

    top_grad = final(row_sum(0), slice(0, 1))
    pg_out[0:1, :] = top_grad
    slope = top_grad / length
    for f in range(n_fsdp):
        scaled = gain_all[f] * slope[:, f * part:(f + 1) * part]
        wide[:, f * part:(f + 1) * part] = jnp.broadcast_to(scaled, (16, part))

    def inner_pass(i, _):
        rows = pl.ds(pl.multiple_of(i * 16, 16), 16)
        acc = h_in[rows, 0:LANES].astype(F32) * wide[:, 0:LANES]
        for l in range(1, dim // LANES):
            cols = slice(l * LANES, (l + 1) * LANES)
            acc = acc + h_in[rows, cols].astype(F32) * wide[:, cols]
        row_coef[rows, :] = acc
        return 0

    lax.fori_loop(0, length // 16, inner_pass, 0, unroll=4)

    shares = share_recv.at[1:half * n_fsdp]
    remote(shares, shares, share_sem.at[0], share_sem.at[1], fsdp=p_mate).wait()
    total = share_send[fsdp].astype(F32)
    for f in range(1, half * n_fsdp):
        total = total + share_recv[f].astype(F32)
    total_all[0] = total
    total_copy = remote(total_all.at[0], total_all.at[1], total_sem.at[0], total_sem.at[1], rep=mate)
    total_copy.start()

    inv = row_inv[...]
    inner = jnp.sum(row_coef[...], axis=-1, keepdims=True)
    row_coef[...] = inner * (inv * inv * inv) / dim

    def last_pass(i, _):
        rows = pl.ds(pl.multiple_of(i * 16, 16), 16)
        inv = row_inv[rows, :]
        coef = row_coef[rows, :]
        for l in range(dim // LANES):
            cols = slice(l * LANES, (l + 1) * LANES)
            h_out[rows, cols] = (wide[:, cols] * inv - h_in[rows, cols].astype(F32) * coef).astype(BF16)
        return 0

    lax.fori_loop(0, length // 16, last_pass, 0, unroll=2)
    pg_out[1:2, :] = final(row_sum(1), slice(1, 2))

    near_copy(0).wait_recv()
    unit_grad = grad_own[0:PAD, :] + near_recv[0].astype(F32)

    total_copy.wait()
    total = total_all[0] + total_all[1]
    gg_out[...] = jnp.concatenate([total[0:1, LANES:], total[1:2, LANES:]], axis=1)
    loss_out[...] = (total[0:1, 0:LANES] + total[1:2, 0:LANES]) / (qry * n_rep * n_fsdp)
    remote(near_send.at[:, 0:rest], near_recv.at[:, 0:rest], near_sent, near_got.at[0],
           fsdp=p_mate).wait_send()

    sums = far_recv.at[1:p_half, 0:rest]
    remote(sums, sums, far_sem.at[0], far_sem.at[1], fsdp=p_mate).wait()
    for k in range(1, p_half):
        unit_grad = unit_grad + far_recv[k].astype(F32)
    pg_out[2:pas, :] = final(unit_grad[0:rest], slice(2, pas))


def write_out(*refs):
    count = (len(refs) - 1) // 2
    sems = refs[-1]
    copies = [pltpu.make_async_copy(refs[i], refs[count + i], sems.at[i]) for i in range(count)]
    for copy in copies:
        copy.start()
    for copy in copies:
        copy.wait()


def per_device(query_cache, passage_cache, positives, norm_gain, hidden_states):
    n_rep, n_fsdp = lax.axis_size("rep"), lax.axis_size("fsdp")
    qry, dim = query_cache.shape
    pas = passage_cache.shape[0]
    length = hidden_states.shape[0]
    part = dim // n_fsdp
    half, p_half = n_rep // 2, n_fsdp // 2
    vmem = pl.BlockSpec(memory_space=pltpu.VMEM)
    hbm = pl.BlockSpec(memory_space=pltpu.HBM)
    dma = pltpu.SemaphoreType.DMA
    results = pl.pallas_call(
        functools.partial(kernel, n_rep, n_fsdp),
        name="step",
        out_shape=(
            pltpu.VMEM((1, LANES), F32),
            pltpu.VMEM((pas, dim), F32),
            pltpu.VMEM((length, dim), BF16),
            pltpu.VMEM((1, part), F32),
        ),
        in_specs=[hbm] * 5,
        out_specs=(vmem, vmem, vmem, vmem),
        scratch_shapes=[
            pltpu.VMEM((qry, dim), BF16),
            pltpu.VMEM((pas, dim), BF16),
            pltpu.VMEM((length, dim), BF16),
            pltpu.VMEM((n_rep, qry, dim), BF16),
            pltpu.VMEM((2 * n_fsdp, PAD, dim), BF16),
            pltpu.VMEM((pas, dim), F32),
            pltpu.VMEM((n_rep, 1, qry), jnp.int32),
            pltpu.VMEM((n_fsdp, 1, part), F32),
            pltpu.VMEM((2, n_fsdp * PAD, half * qry), F32),
            pltpu.VMEM((n_fsdp * PAD, half * qry), F32),
            pltpu.VMEM((n_fsdp * PAD, n_rep * qry), BF16),
            pltpu.VMEM((n_rep, half, 2, LANES), F32),
            pltpu.VMEM((n_fsdp, 2, dim // 2), BF16),
            pltpu.VMEM((2, n_fsdp, 1, dim), F32),
            pltpu.VMEM((2, n_fsdp, 2, dim // 2), BF16),
            pltpu.VMEM((2, n_fsdp, 2, dim // 2), BF16),
            pltpu.VMEM((p_half, PAD, dim), BF16),
            pltpu.VMEM((p_half, PAD, dim), BF16),
            pltpu.VMEM((p_half, PAD, dim), BF16),
            pltpu.VMEM((p_half, PAD, dim), BF16),
            pltpu.VMEM((p_half * PAD, dim), F32),
            pltpu.VMEM((n_fsdp, 2, LANES + part // 2), BF16),
            pltpu.VMEM((half * n_fsdp, 2, LANES + part // 2), BF16),
            pltpu.VMEM((2, 2, LANES + part // 2), F32),
            pltpu.VMEM((8, dim), F32),
            pltpu.VMEM((length, LANES), F32),
            pltpu.VMEM((length, LANES), F32),
            pltpu.VMEM((16, dim), F32),
            dma((4,)), dma((qry // 16,)),
            dma, dma((half - 1, GROUPS)), dma, dma,
            dma, dma((p_half - 1, 2)), dma((p_half, 2)), dma((2,)),
            dma((2,)), dma((2,)), dma((2,)), dma((2,)), dma((2,)), dma((4,)), dma((2,)), dma((2,)),
            dma, dma((p_half,)), dma((2,)),
        ],
        compiler_params=pltpu.CompilerParams(
            collective_id=0, has_side_effects=True, vmem_limit_bytes=40 << 20),
    )(*[pltpu.with_memory_space_constraint(array, pltpu.HBM) for array in (
        query_cache, passage_cache, positives.reshape(1, qry), norm_gain.reshape(1, part),
        hidden_states)])
    loss, passage_grad, hidden_grad, gain_grad = pl.pallas_call(
        write_out,
        name="write_out",
        out_shape=tuple(pltpu.HBM(r.shape, r.dtype) for r in results),
        in_specs=[vmem] * 4,
        out_specs=(hbm,) * 4,
        scratch_shapes=[dma((4,))],
    )(*[pltpu.with_memory_space_constraint(r, pltpu.VMEM) for r in results])
    return loss[0, 0], passage_grad, hidden_grad, gain_grad.reshape(part)


def solution(mesh):
    return jax.shard_map(
        per_device,
        mesh=mesh,
        in_specs=(
            P(("rep", "fsdp"), None),
            P(("rep", "fsdp"), None),
            P(("rep", "fsdp")),
            P("fsdp"),
            P(("rep", "fsdp"), None),
        ),
        out_specs=(P(), P(("rep", "fsdp"), None), P(("rep", "fsdp"), None), P("fsdp")),
        check_vma=False,
    )
```
